32 devices in a mesh: outer: 4 (over x, core), inner: 8 (over z, y).
Axes of the slice: x: 2, y: 2, z: 4, core: 2. Of those that a mesh axis runs over, the one named last changes fastest.
Arguments:
- signal: bfloat16 [4096, 4096], P(('outer', 'inner')), may hold values from -6 to 6
- gating: bfloat16 [4096, 4096], P(('outer', 'inner')), may hold values from -6 to 6
- decay_rate: float32 [4096, 16], P('inner'), may hold values from 0.00012207031 to 0.05
- residues: float32 [4096, 16], P('inner'), may hold values from -1.5 to 1.5
- skip_gain: float32 [4096], replicated, may hold values from -3 to 3
Outputs:
- layer_out: bfloat16 [4096, 4096], P(('outer', 'inner'))
The draws below stay inside these ranges and needn't reach their ends.
All inputs are finite; a program needn't handle non-finite values.
Results may differ from the reference program's by a relative error of at most 0.001.
Values may be sent and summed in bfloat16 or wider, within the bound.
A program may use at most 128 MiB of HBM per device.

```python
import math
import jax
import jax.numpy as jnp
from jax import lax

D = 4096
MODES = 16
TOKENS = 4096


def levels(stream_key, dims, cuts, low, largest):
    def one(axis_at, parts):
        steps = jax.random.uniform(jax.random.fold_in(jax.random.fold_in(stream_key, 6), axis_at), (parts,), jnp.float32, low / len(cuts), largest / len(cuts))
        return jnp.repeat(jnp.exp(steps), dims[axis_at] // parts).reshape((-1,) + (1,) * (len(dims) - axis_at - 1))

    loudness = one(*cuts[0])
    for cut in cuts[1:]:
        loudness = loudness * one(*cut)
    return loudness


def gaussian(stream_key, extent, scale, most, split=(), kind=jnp.bfloat16):
    array = scale * jax.random.normal(stream_key, extent, jnp.float32)
    if split:
        array = array * levels(stream_key, extent, split, -0.22, 0.18)
    return jnp.clip(array, -most, most).astype(kind)


def setup_inputs(seed: int = 0) -> dict:
    streams_of = jax.random.split(jax.random.key(seed), 6)
    return {
        "signal": gaussian(streams_of[0], (TOKENS, D), 1.0, 6.0, ((0, 32),)),
        "gating": gaussian(streams_of[1], (TOKENS, D), 1.0, 6.0, ((0, 32),)),
        "decay_rate": jnp.clip(jnp.exp(math.log(0.05) - 6.015181 * jax.random.uniform(streams_of[2], (D, MODES), jnp.float32) ** levels(streams_of[2], (D, MODES), ((0, 8),), -0.2, 0.2)), 0.00012207031, 0.05),
        "residues": gaussian(streams_of[3], (D, MODES), 0.25, 1.5, ((0, 8),), jnp.float32),
        "skip_gain": gaussian(streams_of[4], (D,), 0.5, 3.0, (), jnp.float32),
    }


def filter_spectrum(frequency, padded, seq_length, decay_rate, residues):
    angles = frequency.astype(jnp.float32) * (2.0 * math.pi / padded)
    sine_half = jnp.sin(0.5 * angles)
    bending = 2.0 * sine_half * sine_half
    sine_full = jnp.sin(angles)
    parity = (1 - 2 * (frequency % 2)).astype(jnp.float32)
    zeros_out = jnp.zeros_like(angles + decay_rate[:, 0])

    def add_mode(mode_index, totals):
        real_sum, imag_sum = totals
        mode_rate = lax.dynamic_index_in_dim(decay_rate, mode_index, 1, keepdims=False)
        weights = lax.dynamic_index_in_dim(residues, mode_index, 1, keepdims=False)
        decays = jnp.exp(-mode_rate)
        scaled = weights * jnp.sqrt(-jnp.expm1(-2.0 * mode_rate))
        numerator = scaled * (1.0 - jnp.exp(-seq_length * mode_rate) * parity)
        den_real = -jnp.expm1(-mode_rate) + decays * bending
        den_imag = decays * sine_full
        quotient = numerator / (den_real * den_real + den_imag * den_imag)
        return (real_sum + quotient * den_real, imag_sum - quotient * den_imag)
    return lax.fori_loop(0, decay_rate.shape[1], add_mode, (zeros_out, zeros_out))

def reference(signal, gating, decay_rate, residues, skip_gain):
    padded = 2 * TOKENS
    block_width = math.gcd(D, 256)
    block_count = D // block_width
    frequency = jnp.arange(padded, dtype=jnp.int32)[:, None]
    signal_f = signal.astype(jnp.float32)
    blocks_in = signal_f.reshape(TOKENS, block_count, block_width).transpose(1, 0, 2)
    rate_blocks = decay_rate.reshape(block_count, block_width, MODES)
    residue_blocks = residues.reshape(block_count, block_width, MODES)

    def convolve(operands):
        block_signal, block_rate, block_residue = operands
        spectrum = jnp.fft.fft(block_signal, n=padded, axis=0)
        filter_re, filter_im = filter_spectrum(frequency, padded, TOKENS, block_rate, block_residue)
        product = spectrum * lax.complex(filter_re, filter_im)
        return jnp.real(jnp.fft.ifft(product, axis=0)[:TOKENS])
    convolved = lax.map(convolve, (blocks_in, rate_blocks, residue_blocks))
    convolved = convolved.transpose(1, 0, 2).reshape(TOKENS, D)
    return (gating.astype(jnp.float32) * (convolved + skip_gain[None, :] * signal_f)).astype(jnp.bfloat16)
```

```python
import functools

import jax
import jax.numpy as jnp
import numpy as np
from jax import lax
from jax.experimental import pallas as pl
from jax.experimental.pallas import tpu as pltpu
from jax.sharding import PartitionSpec as P

MESH = pl.DeviceIdType.MESH
LANES = 128
TILE = 256
F32 = jnp.float32
BF16 = jnp.bfloat16

MOST = 0.05
NODES = 8
NODES_S = (0.00578542, 0.05933078, 0.16499424, 0.31771443,
           0.50753127, 0.70895063, 0.88350275, 0.98635752)
NODES_R = (0.00681489, 0.06128461, 0.17012907, 0.34307065,
           0.48045442, 0.7017412, 0.88152977, 0.98619637)


def wrap(value, size):
    return lax.rem(value + size, size)


def one_minus_exp(z):
    series = jnp.ones_like(z)
    for n in range(12, 1, -1):
        series = 1.0 - series * z * (1.0 / n)
    return jnp.where(z < 0.5, z * series, 1.0 - jnp.exp(-z))


def eliminate(matrix, right):
    matrix, right = matrix.copy(), right.copy()
    size = len(matrix)
    for i in range(size):
        best = i + int(np.argmax(np.abs(matrix[i:, i])))
        matrix[[i, best]], right[[i, best]] = matrix[[best, i]], right[[best, i]]
        for k in range(i + 1, size):
            factor = matrix[k, i] / matrix[i, i]
            matrix[k] -= factor * matrix[i]
            right[k] -= factor * right[i]
    for i in range(size - 1, -1, -1):
        for k in range(i + 1, size):
            right[i] -= matrix[i, k] * right[k]
        right[i] /= matrix[i, i]
    return right


def split(array):
    high = array.astype(jnp.bfloat16)
    low = (array - high.astype(np.float64)).astype(jnp.bfloat16)
    return high, low


def tables(rows):
    assert rows <= 128
    s = np.arange(rows, dtype=np.float64)
    nodes = np.array(NODES_S) * (rows - 1)
    rates = np.array(NODES_R) * MOST
    cards = eliminate(np.exp(-rates[:, None] * nodes), np.exp(-rates[:, None] * s))
    angle = np.pi * (2.0 * s[:, None] + 1.0) / (2.0 * rows) * s[None, :]
    cos, sin = np.cos(angle), np.sin(angle)
    forward = np.concatenate([cos, -sin])
    inverse = np.concatenate([cos.T, -sin.T], axis=1) / rows
    taps = np.zeros((16, rows))
    taps[:NODES] = cards
    taps[NODES, 0] = 1.0
    response = forward @ taps.T
    ends = np.zeros((8, rows))
    ends[:NODES] = cards[:, ::-1]
    carry = np.zeros((rows, 16))
    carry[:, :NODES] = cards.T
    f_high, f_low = split(forward)
    r_high, r_low = split(response)
    i_high, i_low = split(inverse)
    e_high, e_low = split(ends)
    c_high, c_low = split(carry)
    node_rows = np.repeat(nodes[:, None], LANES, axis=1).astype(np.float32)
    return nodes, (
        np.concatenate([f_high, f_low], axis=1),
        np.concatenate([r_high, r_high, r_low], axis=1),
        np.concatenate([i_high, i_low]),
        np.concatenate([e_high, e_low]),
        np.concatenate([c_high, c_high, c_low], axis=1),
        node_rows,
    )


def pieces(value):
    high = value.astype(BF16)
    return high, (value - high.astype(F32)).astype(BF16)


def dot(a, b):
    return jnp.dot(a, b, preferred_element_type=F32)


def kernel(
    groups, inner, modes, nodes,
    rate_hbm, residue_hbm, signal_hbm, gating_hbm, skip_hbm,
    forward_hbm, response_hbm, inverse_hbm, ends_hbm, carry_hbm, node_hbm, out_hbm,
    rate_ref, residue_ref, signal_ref, gating_ref, skip_ref,
    forward_ref, response_ref, inverse_ref, ends_ref, carry_ref, node_ref,
    out_buf, y_buf, phi_buf, wphi_buf, taps_buf, part_out, part_got, local_buf, value_out,
    value_got, total_buf, row_buf,
    load_sem, out_sem, taps_send, taps_recv, relay_send, part_send, part_recv,
    value_send, value_recv, total_send, total_recv,
):
    me = lax.axis_index("inner")
    block = lax.axis_index("outer")
    rows, channels = signal_ref.shape
    width = rate_ref.shape[1]
    tile = min(TILE, width)

    barrier = pltpu.get_barrier_semaphore()

    @pl.loop(1, inner)
    def _(r):
        pl.semaphore_signal(
            barrier, inc=1, device_id={"inner": wrap(me + r, inner)}, device_id_type=MESH
        )

    @pl.loop(1, groups)
    def _(r):
        pl.semaphore_signal(
            barrier, inc=1, device_id={"outer": wrap(block + r, groups)}, device_id_type=MESH
        )

    loads = [
        pltpu.make_async_copy(source, target, load_sem.at[n])
        for n, (source, target) in enumerate((
            (rate_hbm, rate_ref), (residue_hbm, residue_ref), (node_hbm, node_ref),
            (ends_hbm, ends_ref), (signal_hbm, signal_ref),
            (forward_hbm, forward_ref), (response_hbm, response_ref),
            (inverse_hbm, inverse_ref), (skip_hbm, skip_ref), (carry_hbm, carry_ref),
            (gating_hbm, gating_ref),
        ))
    ]
    for load in loads:
        load.start()

    def remote(source, target, send, recv, device):
        return pltpu.make_async_remote_copy(
            src_ref=source, dst_ref=target, send_sem=send, recv_sem=recv,
            device_id=device, device_id_type=MESH,
        )

    def taps_copy(r):
        return remote(
            taps_buf.at[0], taps_buf.at[r],
            taps_send.at[r], taps_recv.at[r], {"inner": wrap(me + r, inner)},
        )

    def relay_copy(r, d):
        return remote(
            taps_buf.at[r], taps_buf.at[r],
            relay_send.at[r, d], taps_recv.at[r], {"outer": wrap(block + d, groups)},
        )

    def part_copy(r):
        return remote(
            part_out.at[r], part_got.at[r],
            part_send.at[r], part_recv.at[r], {"inner": wrap(me - r, inner)},
        )

    def value_copy(r):
        return remote(
            value_out.at[r], value_got.at[r],
            value_send.at[r], value_recv.at[r], {"inner": wrap(me + r, inner)},
        )

    def total_copy(r):
        return remote(
            total_buf.at[0], total_buf.at[r],
            total_send.at[r], total_recv.at[r], {"outer": wrap(block + r, groups)},
        )

    def out_copy(slot):
        start = wrap(me - slot, inner) * width
        cols = pl.ds(pl.multiple_of(start, LANES), width)
        return pltpu.make_async_copy(
            out_buf.at[:, cols], out_hbm.at[:, cols], out_sem.at[slot]
        )

    def place(slot, at=0, size=width):
        start = wrap(me - slot, inner) * width + at
        return pl.ds(pl.multiple_of(start, LANES), size)

    for n in range(3):
        loads[n].wait()
    rate = rate_ref[...]
    for j in range(NODES):
        phi_buf[j] = jnp.exp(rate * (-float(nodes[j])))
    row_buf[...] = residue_ref[...] * jnp.sqrt(one_minus_exp(2.0 * rate))
    node_col = jnp.concatenate([node_ref[...]] * (width // LANES), axis=1)
    taps = jnp.zeros((NODES, width), F32)
    for m in range(modes):
        value = row_buf[m : m + 1, :] * jnp.exp(-(rate_ref[m : m + 1, :] * node_col))
        wphi_buf[m] = value
        taps = taps + value
    taps_buf[0] = taps
    pl.semaphore_wait(barrier, inner + groups - 2)

    def mine(r):
        return lax.rem(r, groups) == block

    @pl.loop(1, inner)
    def _(r):
        @pl.when(mine(r))
        def _():
            taps_copy(r).start()

    loads[3].wait()
    loads[4].wait()

    @pl.loop(1, inner + 1)
    def _(step):
        r = lax.rem(step, inner)
        both = dot(ends_ref[...], signal_ref[:, place(r)])
        part_out[r] = both[:NODES] + both[NODES:]

        @pl.when(r > 0)
        def _():
            part_copy(r).start()

    def relay(r):
        @pl.when(mine(r))
        def _():
            taps_copy(r).wait_recv()

            @pl.loop(1, groups)
            def _(d):
                relay_copy(r, d).start()

    for n in range(5, 9):
        loads[n].wait()

    def local(r):
        for at in range(0, width, tile):
            cols = place(r, at, tile)
            signal = signal_ref[:, cols]
            spectrum = dot(forward_ref[...], jnp.concatenate([signal, signal]))
            filters = jnp.concatenate([
                taps_buf[r, :, at : at + tile], skip_ref[:, cols],
                jnp.zeros((7, tile), F32),
            ])
            high, low = pieces(filters)
            response = dot(response_ref[...], jnp.concatenate([high, low, high]))
            s_re, s_im = spectrum[:rows], spectrum[rows:]
            r_re, r_im = response[:rows], response[rows:]
            product = jnp.concatenate([
                s_re * r_re - s_im * r_im, s_re * r_im + s_im * r_re,
            ])
            high, low = pieces(product)
            two = dot(inverse_ref[...], high)
            one = dot(inverse_ref[:rows], low)
            y_buf[:, cols] = two[:rows] + (two[rows:] + one)

    local(0)

    @pl.loop(1, inner)
    def _(r):
        relay(r)

    @pl.loop(1, inner)
    def _(r):
        part_copy(r).wait_recv()

    part_got[0] = part_out[0]
    decay_block = jnp.exp(rate * (-float(rows)))

    def advance(b, run):
        at = wrap(b - me, inner)
        local_buf[at] = run
        run = decay_block * run
        for j in range(NODES):
            run = run + phi_buf[j] * part_got[at, j : j + 1, :]
        return run

    nothing = jnp.zeros((modes, width), F32)
    total_buf[0] = lax.fori_loop(0, inner, advance, nothing)

    @pl.loop(1, groups)
    def _(r):
        total_copy(r).start()

    @pl.loop(1, inner // 2)
    def _(r):
        @pl.when(jnp.logical_not(mine(r)))
        def _():
            taps_copy(r).wait_recv()

        local(r)

    @pl.loop(1, groups)
    def _(r):
        total_copy(r).wait_recv()

    rate = rate_ref[...]
    decay_group = jnp.exp(rate * (-float(rows * inner)))

    def join(b, run):
        got = total_buf[wrap(block - b, groups)]
        return jnp.where(b < block, decay_group * run + got, run)

    before = lax.fori_loop(0, groups, join, nothing)
    row_buf[...] = before

    @pl.loop(1, inner + 1)
    def _(step):
        r = lax.rem(step, inner)
        b = wrap(me + r, inner)
        reach = (b * (-rows)).astype(F32) - 1.0
        rate = rate_ref[...]
        local_buf[r] = (
            jnp.exp(-rate) * local_buf[r] + jnp.exp(rate * reach) * row_buf[...]
        )
        value = jnp.zeros((NODES, width), F32)
        for m in range(modes):
            value = value + wphi_buf[m] * local_buf[r, m : m + 1, :]
        value_out[r] = value

        @pl.when(r > 0)
        def _():
            value_copy(r).start()

    value_got[0] = value_out[0]

    @pl.loop(inner // 2, inner)
    def _(r):
        @pl.when(jnp.logical_not(mine(r)))
        def _():
            taps_copy(r).wait_recv()

        local(r)

    loads[9].wait()
    loads[10].wait()

    @pl.loop(0, inner)
    def _(r):
        @pl.when(r > 0)
        def _():
            value_copy(r).wait_recv()

        for at in range(0, width, tile):
            cols = place(r, at, tile)
            value = value_got[r, :, at : at + tile]
            high, low = pieces(jnp.concatenate([value, jnp.zeros_like(value)]))
            carried = dot(carry_ref[...], jnp.concatenate([high, low, high]))
            gate = gating_ref[:, cols].astype(F32)
            out_buf[:, cols] = (gate * (y_buf[:, cols] + carried)).astype(BF16)
        out_copy(r).start()

    @pl.loop(1, inner)
    def _(r):
        part_copy(r).wait_send()
        value_copy(r).wait_send()

        @pl.when(mine(r))
        def _():
            taps_copy(r).wait_send()

            @pl.loop(1, groups)
            def _(d):
                relay_copy(r, d).wait_send()

    @pl.loop(1, groups)
    def _(r):
        total_copy(r).wait_send()

    @pl.loop(0, inner)
    def _(r):
        out_copy(r).wait()


def per_device(signal, gating, decay_rate, residues, skip_gain):
    groups = lax.axis_size("outer")
    inner = lax.axis_size("inner")
    rows, channels = signal.shape
    width, modes = decay_rate.shape
    dma = pltpu.SemaphoreType.DMA
    nodes, constants = tables(rows)
    arguments = (
        decay_rate.T, residues.T, signal, gating, skip_gain[None, :],
        *[jnp.asarray(c) for c in constants],
    )
    node_rows = pltpu.VMEM((inner, NODES, width), F32)
    mode_rows = pltpu.VMEM((modes, width), F32)

    return pl.pallas_call(
        functools.partial(kernel, groups, inner, modes, nodes),
        out_shape=jax.ShapeDtypeStruct((rows, channels), BF16),
        in_specs=[pl.BlockSpec(memory_space=pltpu.HBM)] * len(arguments),
        out_specs=pl.BlockSpec(memory_space=pltpu.HBM),
        scratch_shapes=[
            *[pltpu.VMEM(a.shape, a.dtype) for a in arguments],
            pltpu.VMEM((rows, channels), BF16),
            pltpu.VMEM((rows, channels), F32),
            pltpu.VMEM((NODES, modes, width), F32),
            pltpu.VMEM((modes, NODES, width), F32),
            node_rows, node_rows, node_rows,
            pltpu.VMEM((inner, modes, width), F32),
            node_rows, node_rows,
            pltpu.VMEM((groups, modes, width), F32),
            mode_rows,
            dma((len(arguments),)), dma((inner,)),
            dma((inner,)), dma((inner,)), dma((inner, groups)),
            dma((inner,)), dma((inner,)), dma((inner,)), dma((inner,)),
            dma((groups,)), dma((groups,)),
        ],
        compiler_params=pltpu.CompilerParams(
            collective_id=0, has_side_effects=True, vmem_limit_bytes=56 * 1024 * 1024
        ),
        name="modal_scan",
    )(*arguments)


def solution(mesh):
    return jax.shard_map(
        per_device,
        mesh=mesh,
        in_specs=(
            P(("outer", "inner"), None),
            P(("outer", "inner"), None),
            P("inner", None),
            P("inner", None),
            P(),
        ),
        out_specs=P(("outer", "inner"), None),
        check_vma=False,
    )
```

```python
import functools

import jax
import jax.numpy as jnp
import numpy as np
from jax import lax
from jax.experimental import pallas as pl
from jax.experimental.pallas import tpu as pltpu
from jax.sharding import PartitionSpec as P

MESH = pl.DeviceIdType.MESH
LANES = 128
TILE = 256
F32 = jnp.float32
BF16 = jnp.bfloat16

MOST = 0.05
NODES = 8
NODES_S = (0.00578542, 0.05933078, 0.16499424, 0.31771443,
           0.50753127, 0.70895063, 0.88350275, 0.98635752)
NODES_R = (0.00681489, 0.06128461, 0.17012907, 0.34307065,
           0.48045442, 0.7017412, 0.88152977, 0.98619637)


def wrap(value, size):
    return lax.rem(value + size, size)


def one_minus_exp(z):
    series = jnp.ones_like(z)
    for n in range(12, 1, -1):
        series = 1.0 - series * z * (1.0 / n)
    return jnp.where(z < 0.5, z * series, 1.0 - jnp.exp(-z))


def eliminate(matrix, right):
    matrix, right = matrix.copy(), right.copy()
    size = len(matrix)
    for i in range(size):
        best = i + int(np.argmax(np.abs(matrix[i:, i])))
        matrix[[i, best]], right[[i, best]] = matrix[[best, i]], right[[best, i]]
        for k in range(i + 1, size):
            factor = matrix[k, i] / matrix[i, i]
            matrix[k] -= factor * matrix[i]
            right[k] -= factor * right[i]
    for i in range(size - 1, -1, -1):
        for k in range(i + 1, size):
            right[i] -= matrix[i, k] * right[k]
        right[i] /= matrix[i, i]
    return right


def split(array):
    high = array.astype(jnp.bfloat16)
    low = (array - high.astype(np.float64)).astype(jnp.bfloat16)
    return high, low


def tables(rows):
    assert rows <= 128
    s = np.arange(rows, dtype=np.float64)
    nodes = np.array(NODES_S) * (rows - 1)
    rates = np.array(NODES_R) * MOST
    cards = eliminate(np.exp(-rates[:, None] * nodes), np.exp(-rates[:, None] * s))
    angle = np.pi * (2.0 * s[:, None] + 1.0) / (2.0 * rows) * s[None, :]
    cos, sin = np.cos(angle), np.sin(angle)
    forward = np.concatenate([cos, -sin])
    inverse = np.concatenate([cos.T, -sin.T], axis=1) / rows
    taps = np.zeros((16, rows))
    taps[:NODES] = cards
    taps[NODES, 0] = 1.0
    response = forward @ taps.T
    ends = np.zeros((8, rows))
    ends[:NODES] = cards[:, ::-1]
    carry = np.zeros((rows, 16))
    carry[:, :NODES] = cards.T
    f_high, f_low = split(forward)
    r_high, r_low = split(response)
    i_high, i_low = split(inverse)
    e_high, e_low = split(ends)
    c_high, c_low = split(carry)
    node_rows = np.repeat(nodes[:, None], LANES, axis=1).astype(np.float32)
    return nodes, (
        np.concatenate([f_high, f_low], axis=1),
        np.concatenate([r_high, r_high, r_low], axis=1),
        np.concatenate([i_high, i_low]),
        np.concatenate([e_high, e_low]),
        np.concatenate([c_high, c_high, c_low], axis=1),
        node_rows,
    )


def pieces(value):
    high = value.astype(BF16)
    return high, (value - high.astype(F32)).astype(BF16)


def dot(a, b):
    return jnp.dot(a, b, preferred_element_type=F32)


def kernel(
    groups, inner, owners, modes, nodes,
    rate_hbm, residue_hbm, signal_hbm, gating_hbm, skip_hbm,
    forward_hbm, response_hbm, inverse_hbm, ends_hbm, carry_hbm, node_hbm, out_hbm,
    rate_ref, residue_ref, signal_ref, gating_ref, skip_ref,
    forward_ref, response_ref, inverse_ref, ends_ref, carry_ref, node_ref,
    out_buf, y_buf, x_buf, phi_buf, wphi_buf, taps_buf, part_out, part_got, state_buf,
    value_out, value_got, row_buf,
    load_sem, out_sem, taps_send, taps_recv, relay_send, part_send, part_recv,
    value_send, value_recv,
):
    me = lax.axis_index("inner")
    block = lax.axis_index("outer")
    half = lax.rem(block, 2)
    twin = block + 1 - 2 * half
    rows, channels = signal_ref.shape
    width = rate_ref.shape[1]
    share = width // owners
    tile = min(TILE, width)
    blocks = groups * inner
    here = block * inner + me
    owns = block < owners
    own_cols = pl.ds(pl.multiple_of(lax.rem(block, owners) * share, LANES), share)

    barrier = pltpu.get_barrier_semaphore()

    @pl.loop(0, blocks)
    def _(p):
        @pl.when(p != here)
        def _():
            pl.semaphore_signal(
                barrier, inc=1, device_id={"outer": p // inner, "inner": p % inner},
                device_id_type=MESH,
            )

    loads = [
        pltpu.make_async_copy(source, target, load_sem.at[n])
        for n, (source, target) in enumerate((
            (rate_hbm, rate_ref), (residue_hbm, residue_ref), (node_hbm, node_ref),
            (ends_hbm, ends_ref), (signal_hbm, signal_ref),
            (forward_hbm, forward_ref), (response_hbm, response_ref),
            (inverse_hbm, inverse_ref), (skip_hbm, skip_ref), (carry_hbm, carry_ref),
            (gating_hbm, gating_ref),
        ))
    ]
    for load in loads:
        load.start()

    def remote(source, target, send, recv, device):
        return pltpu.make_async_remote_copy(
            src_ref=source, dst_ref=target, send_sem=send, recv_sem=recv,
            device_id=device, device_id_type=MESH,
        )

    def taps_copy(r):
        return remote(
            taps_buf.at[0], taps_buf.at[r],
            taps_send.at[r], taps_recv.at[r], {"inner": wrap(me + r, inner)},
        )

    def relay_copy(r):
        return remote(
            taps_buf.at[r], taps_buf.at[r],
            relay_send.at[r], taps_recv.at[r], {"outer": twin},
        )

    def part_copy(owner, source):
        return remote(
            part_out.at[owner], part_got.at[source],
            part_send.at[owner], part_recv.at[source],
            {"outer": owner // inner, "inner": owner % inner},
        )

    def value_copy(target, owner):
        return remote(
            value_out.at[target], value_got.at[owner],
            value_send.at[target], value_recv.at[owner],
            {"outer": target // inner, "inner": target % inner},
        )

    def out_copy(slot):
        cols = place(slot)
        return pltpu.make_async_copy(
            out_buf.at[:, cols], out_hbm.at[:, cols], out_sem.at[slot]
        )

    def place(slot, at=0, size=width):
        start = wrap(me - slot, inner) * width + at
        return pl.ds(pl.multiple_of(start, LANES), size)

    for n in range(3):
        loads[n].wait()
    own_rate = rate_ref[:, own_cols]
    for j in range(NODES):
        phi_buf[j] = jnp.exp(own_rate * (-float(nodes[j])))
    row_buf[...] = residue_ref[...] * jnp.sqrt(one_minus_exp(2.0 * rate_ref[...]))
    node_col = jnp.concatenate([node_ref[...]] * (width // LANES), axis=1)
    taps = jnp.zeros((NODES, width), F32)
    for m in range(modes):
        value = row_buf[m : m + 1, :] * jnp.exp(-(rate_ref[m : m + 1, :] * node_col))
        wphi_buf[m] = value
        taps = taps + value
    taps_buf[0] = taps
    pl.semaphore_wait(barrier, blocks - 1)

    def mine(r):
        return lax.rem(r, 2) == half

    loads[3].wait()
    loads[4].wait()

    @pl.loop(1, inner + 1)
    def _(step):
        i = wrap(me + step, inner)
        cols = pl.ds(pl.multiple_of(i * width, LANES), width)
        both = dot(ends_ref[...], signal_ref[:, cols])
        part = both[:NODES] + both[NODES:]
        for g in range(owners):
            owner = g * inner + i
            part_out[owner] = part[:, g * share : (g + 1) * share]

            @pl.when(owner != here)
            def _():
                part_copy(owner, here).start()

        @pl.when(jnp.logical_and(step < inner, mine(step)))
        def _():
            taps_copy(step).start()

    for n in range(5, 9):
        loads[n].wait()

    @pl.loop(0, channels // tile)
    def _(n):
        cols = pl.ds(pl.multiple_of(n * tile, LANES), tile)
        signal = signal_ref[:, cols]
        x_buf[:, cols] = dot(forward_ref[...], jnp.concatenate([signal, signal]))

    @pl.when(owns)
    def _():
        part_got[here] = part_out[here]
        own_rate = rate_ref[:, own_cols]
        decay_block = jnp.exp(own_rate * (-float(rows)))
        decay_one = jnp.exp(-own_rate)

        def advance(p, run):
            @pl.when(p != here)
            def _():
                part_copy(0, p).wait_recv()

            state_buf[p] = decay_one * run
            ends = [phi_buf[j] * part_got[p, j : j + 1, :] for j in range(NODES)]
            while len(ends) > 1:
                ends = [a + b for a, b in zip(ends[::2], ends[1::2])]
            return decay_block * run + ends[0]

        lax.fori_loop(0, blocks, advance, jnp.zeros((modes, share), F32))

        @pl.loop(1, blocks)
        def _(p):
            terms = [
                wphi_buf[m, :, own_cols] * state_buf[p, m : m + 1, :] for m in range(modes)
            ]
            while len(terms) > 1:
                terms = [a + b for a, b in zip(terms[::2], terms[1::2])]
            value_out[p] = terms[0]

            @pl.when(p != here)
            def _():
                value_copy(p, here).start()

        @pl.when(here > 0)
        def _():
            value_got[here] = value_out[here]

    @pl.loop(1, inner)
    def _(r):
        @pl.when(mine(r))
        def _():
            taps_copy(r).wait_recv()
            relay_copy(r).start()

    def local(r):
        for at in range(0, width, tile):
            cols = place(r, at, tile)
            filters = jnp.concatenate([
                taps_buf[r, :, at : at + tile], skip_ref[:, cols],
                jnp.zeros((7, tile), F32),
            ])
            high, low = pieces(filters)
            response = dot(response_ref[...], jnp.concatenate([high, low, high]))
            s_re, s_im = x_buf[:rows, cols], x_buf[rows:, cols]
            r_re, r_im = response[:rows], response[rows:]
            product = jnp.concatenate([
                s_re * r_re - s_im * r_im, s_re * r_im + s_im * r_re,
            ])
            high, low = pieces(product)
            two = dot(inverse_ref[...], high)
            one = dot(inverse_ref[:rows], low)
            y_buf[:, cols] = two[:rows] + (two[rows:] + one)

    @pl.loop(0, inner // 2)
    def _(k):
        local(2 * k + half)

    @pl.loop(0, inner // 2)
    def _(k):
        r = 2 * k + 1 - half

        @pl.when(r > 0)
        def _():
            taps_copy(r).wait_recv()

        local(r)

    loads[9].wait()
    loads[10].wait()

    @pl.when(here == 0)
    def _():
        value_got[...] = jnp.zeros_like(value_got)

    @pl.loop(0, inner)
    def _(r):
        i = wrap(me - r, inner)
        for g in range(owners):
            owner = g * inner + i

            @pl.when(jnp.logical_and(here > 0, owner != here))
            def _():
                value_copy(0, owner).wait_recv()

        value = jnp.concatenate(
            [value_got[g * inner + i] for g in range(owners)], axis=1
        )
        for at in range(0, width, tile):
            cols = place(r, at, tile)
            part = value[:, at : at + tile]
            high, low = pieces(jnp.concatenate([part, jnp.zeros_like(part)]))
            carried = dot(carry_ref[...], jnp.concatenate([high, low, high]))
            gate = gating_ref[:, cols].astype(F32)
            out_buf[:, cols] = (gate * (y_buf[:, cols] + carried)).astype(BF16)
        out_copy(r).start()

    @pl.loop(1, inner)
    def _(r):
        @pl.when(mine(r))
        def _():
            taps_copy(r).wait_send()
            relay_copy(r).wait_send()

    @pl.loop(0, owners * inner)
    def _(owner):
        @pl.when(owner != here)
        def _():
            part_copy(owner, here).wait_send()

    @pl.loop(1, blocks)
    def _(p):
        @pl.when(jnp.logical_and(owns, p != here))
        def _():
            value_copy(p, here).wait_send()

    @pl.loop(0, inner)
    def _(r):
        out_copy(r).wait()


def per_device(signal, gating, decay_rate, residues, skip_gain):
    groups = lax.axis_size("outer")
    inner = lax.axis_size("inner")
    rows, channels = signal.shape
    width, modes = decay_rate.shape
    owners = max(1, min(groups, width // LANES))
    share = width // owners
    blocks = groups * inner
    dma = pltpu.SemaphoreType.DMA
    nodes, constants = tables(rows)
    arguments = (
        decay_rate.T, residues.T, signal, gating, skip_gain[None, :],
        *[jnp.asarray(c) for c in constants],
    )

    return pl.pallas_call(
        functools.partial(kernel, groups, inner, owners, modes, nodes),
        out_shape=jax.ShapeDtypeStruct((rows, channels), BF16),
        in_specs=[pl.BlockSpec(memory_space=pltpu.HBM)] * len(arguments),
        out_specs=pl.BlockSpec(memory_space=pltpu.HBM),
        scratch_shapes=[
            *[pltpu.VMEM(a.shape, a.dtype) for a in arguments],
            pltpu.VMEM((rows, channels), BF16),
            pltpu.VMEM((rows, channels), F32),
            pltpu.VMEM((2 * rows, channels), F32),
            pltpu.VMEM((NODES, modes, share), F32),
            pltpu.VMEM((modes, NODES, width), F32),
            pltpu.VMEM((inner, NODES, width), F32),
            pltpu.VMEM((owners * inner, NODES, share), F32),
            pltpu.VMEM((blocks, NODES, share), F32),
            pltpu.VMEM((blocks, modes, share), F32),
            pltpu.VMEM((blocks, NODES, share), F32),
            pltpu.VMEM((owners * inner, NODES, share), F32),
            pltpu.VMEM((modes, width), F32),
            dma((len(arguments),)), dma((inner,)),
            dma((inner,)), dma((inner,)), dma((inner,)),
            dma((owners * inner,)), dma((blocks,)), dma((blocks,)), dma((owners * inner,)),
        ],
        compiler_params=pltpu.CompilerParams(
            collective_id=0, has_side_effects=True, vmem_limit_bytes=56 * 1024 * 1024
        ),
        name="modal_scan",
    )(*arguments)


def solution(mesh):
    return jax.shard_map(
        per_device,
        mesh=mesh,
        in_specs=(
            P(("outer", "inner"), None),
            P(("outer", "inner"), None),
            P("inner", None),
            P("inner", None),
            P(),
        ),
        out_specs=P(("outer", "inner"), None),
        check_vma=False,
    )
```

```python
import functools

import jax
import jax.numpy as jnp
import numpy as np
from jax import lax
from jax.experimental import pallas as pl
from jax.experimental.pallas import tpu as pltpu
from jax.sharding import PartitionSpec as P

MESH = pl.DeviceIdType.MESH
LANES = 128
F32 = jnp.float32
BF16 = jnp.bfloat16

MOST = 0.05
NODES = 8
NODES_S = (0.00578542, 0.05933078, 0.16499424, 0.31771443,
           0.50753127, 0.70895063, 0.88350275, 0.98635752)
NODES_R = (0.00681489, 0.06128461, 0.17012907, 0.34307065,
           0.48045442, 0.7017412, 0.88152977, 0.98619637)


def wrap(value, size):
    return lax.rem(value + size, size)


def one_minus_exp(z):
    series = jnp.ones_like(z)
    for n in range(12, 1, -1):
        series = 1.0 - series * z * (1.0 / n)
    return jnp.where(z < 0.5, z * series, 1.0 - jnp.exp(-z))


def eliminate(matrix, right):
    matrix, right = matrix.copy(), right.copy()
    size = len(matrix)
    for i in range(size):
        best = i + int(np.argmax(np.abs(matrix[i:, i])))
        matrix[[i, best]], right[[i, best]] = matrix[[best, i]], right[[best, i]]
        for k in range(i + 1, size):
            factor = matrix[k, i] / matrix[i, i]
            matrix[k] -= factor * matrix[i]
            right[k] -= factor * right[i]
    for i in range(size - 1, -1, -1):
        for k in range(i + 1, size):
            right[i] -= matrix[i, k] * right[k]
        right[i] /= matrix[i, i]
    return right


def split(array):
    high = array.astype(jnp.bfloat16)
    low = (array - high.astype(np.float64)).astype(jnp.bfloat16)
    return high, low


def tables(rows):
    assert rows <= 128
    s = np.arange(rows, dtype=np.float64)
    nodes = np.array(NODES_S) * (rows - 1)
    rates = np.array(NODES_R) * MOST
    cards = eliminate(np.exp(-rates[:, None] * nodes), np.exp(-rates[:, None] * s))
    angle = np.pi * (2.0 * s[:, None] + 1.0) / (2.0 * rows) * s[None, :]
    cos, sin = np.cos(angle), np.sin(angle)
    forward = np.concatenate([cos, -sin])
    inverse = np.concatenate([cos.T, -sin.T], axis=1) / rows
    taps = np.zeros((16, rows))
    taps[:NODES] = cards
    taps[NODES, 0] = 1.0
    response = forward @ taps.T
    ends = np.zeros((8, rows))
    ends[:NODES] = cards[:, ::-1]
    carry = np.zeros((rows, 16))
    carry[:, :NODES] = cards.T
    f_high, f_low = split(forward)
    r_high, r_low = split(response)
    i_high, i_low = split(inverse)
    e_high, e_low = split(ends)
    c_high, c_low = split(carry)
    node_rows = np.repeat(nodes[:, None], LANES, axis=1).astype(np.float32)
    return nodes, (
        np.concatenate([f_high, f_low], axis=1),
        np.concatenate([r_high, r_high, r_low], axis=1),
        np.concatenate([i_high, i_low]),
        np.concatenate([e_high, e_low]),
        np.concatenate([c_high, c_high, c_low], axis=1),
        node_rows,
    )


def pieces(value):
    high = value.astype(BF16)
    return high, (value - high.astype(F32)).astype(BF16)


def dot(a, b):
    return jnp.dot(a, b, preferred_element_type=F32)


def kernel(
    groups, inner, owners, modes, nodes,
    rate_hbm, residue_hbm, signal_hbm, gating_hbm, skip_hbm,
    forward_hbm, response_hbm, inverse_hbm, ends_hbm, carry_hbm, node_hbm, out_hbm,
    rate_ref, residue_ref, signal_ref, gating_ref, skip_ref,
    forward_ref, response_ref, inverse_ref, ends_ref, carry_ref, node_ref,
    out_buf, y_buf, phi_buf, wphi_buf, taps_own, taps_buf, part_out, part_got, state_buf,
    value_out, value_got, row_buf,
    load_sem, out_sem, taps_send, taps_recv, relay_send, relay_recv, part_send, part_recv,
    value_send, value_recv,
):
    me = lax.axis_index("inner")
    block = lax.axis_index("outer")
    half = lax.rem(block, 2)
    twin = block + 1 - 2 * half
    rows, channels = signal_ref.shape
    width = rate_ref.shape[1]
    share = width // owners
    blocks = groups * inner
    here = block * inner + me
    owns = block < owners
    own_cols = pl.ds(pl.multiple_of(lax.rem(block, owners) * share, LANES), share)

    order = sorted(range(inner), key=lambda r: abs(r - inner // 2))

    def others():
        for r in order:
            for g in range(groups):
                if r or g:
                    yield wrap(block + g, groups), wrap(me + r, inner)

    barrier = pltpu.get_barrier_semaphore()
    for g, i in others():
        pl.semaphore_signal(
            barrier, inc=1, device_id={"outer": g, "inner": i}, device_id_type=MESH
        )

    loads = [
        pltpu.make_async_copy(source, target, load_sem.at[n])
        for n, (source, target) in enumerate((
            (rate_hbm, rate_ref), (residue_hbm, residue_ref), (node_hbm, node_ref),
            (ends_hbm, ends_ref), (signal_hbm, signal_ref),
            (forward_hbm, forward_ref), (response_hbm, response_ref),
            (inverse_hbm, inverse_ref), (skip_hbm, skip_ref), (carry_hbm, carry_ref),
            (gating_hbm, gating_ref),
        ))
    ]
    for load in loads:
        load.start()

    def remote(source, target, send, recv, device):
        return pltpu.make_async_remote_copy(
            src_ref=source, dst_ref=target, send_sem=send, recv_sem=recv,
            device_id=device, device_id_type=MESH,
        )

    def taps_copy(source, i):
        return remote(
            taps_own, taps_buf.at[source % 2, source // 2],
            taps_send.at[i], taps_recv.at[source], {"inner": i},
        )

    def relay_copy(parity):
        return remote(
            taps_buf.at[parity], taps_buf.at[parity],
            relay_send, relay_recv, {"outer": twin},
        )

    def part_copy(g, i, source):
        return remote(
            part_out.at[i * owners + g], part_got.at[source],
            part_send.at[i * owners + g], part_recv.at[source], {"outer": g, "inner": i},
        )

    def value_copy(g, i, source):
        return remote(
            value_out.at[g * inner + i], value_got.at[source],
            value_send.at[g * inner + i], value_recv.at[source], {"outer": g, "inner": i},
        )

    def stretch(n):
        size = channels // 2
        return pl.ds(pl.multiple_of(n * size, LANES), size)

    def out_copy(n):
        return pltpu.make_async_copy(
            out_buf.at[:, stretch(n)], out_hbm.at[:, stretch(n)], out_sem.at[n]
        )

    for n in range(3):
        loads[n].wait()
    own_rate = rate_ref[:, own_cols]
    for j in range(NODES):
        phi_buf[j] = jnp.exp(own_rate * (-float(nodes[j])))
    row_buf[...] = residue_ref[...] * jnp.sqrt(one_minus_exp(2.0 * rate_ref[...]))
    node_col = jnp.concatenate([node_ref[...]] * (width // LANES), axis=1)
    taps = jnp.zeros((NODES, width), F32)
    for m in range(modes):
        value = row_buf[m : m + 1, :] * jnp.exp(-(rate_ref[m : m + 1, :] * node_col))
        wphi_buf[m] = value
        taps = taps + value
    taps_own[...] = taps
    parity = lax.rem(half + me, 2)

    @pl.when(half == 0)
    def _():
        taps_buf[parity, me // 2] = taps

    loads[3].wait()
    loads[4].wait()
    for n in range(2):
        both = dot(ends_ref[...], signal_ref[:, n * channels // 2 : (n + 1) * channels // 2])
        part = both[:NODES] + both[NODES:]
        for k in range(owners * inner // 2):
            part_out[n * owners * inner // 2 + k] = part[:, k * share : (k + 1) * share]

    pl.semaphore_wait(barrier, blocks - 1)

    if owners == groups:
        for g, i in others():
            part_copy(g, i, here).start()
    else:
        for r in order:
            for g in range(owners):
                @pl.when(jnp.logical_or(r > 0, block != g))
                def _():
                    part_copy(g, wrap(me + r, inner), here).start()

    def mine(i):
        return jnp.logical_and(lax.rem(i + me, 2) == half, i != me)

    @pl.loop(0, inner)
    def _(i):
        @pl.when(mine(i))
        def _():
            taps_copy(me, i).start()

    @pl.when(owns)
    def _():
        part_got[here] = part_out[me * owners + block]
        own_rate = rate_ref[:, own_cols]
        decay_block = jnp.exp(own_rate * (-float(rows)))
        decay_one = jnp.exp(-own_rate)

        def advance(p, run):
            @pl.when(p != here)
            def _():
                part_copy(0, 0, p).wait_recv()

            state_buf[p] = decay_one * run
            ends = [phi_buf[j] * part_got[p, j : j + 1, :] for j in range(NODES)]
            while len(ends) > 1:
                ends = [a + b for a, b in zip(ends[::2], ends[1::2])]
            return decay_block * run + ends[0]

        lax.fori_loop(0, blocks, advance, jnp.zeros((modes, share), F32), unroll=4)

        @pl.loop(0, blocks, unroll=8)
        def _(p):
            terms = [
                wphi_buf[m, :, own_cols] * state_buf[p, m : m + 1, :] for m in range(modes)
            ]
            while len(terms) > 1:
                terms = [a + b for a, b in zip(terms[::2], terms[1::2])]
            value_out[p] = terms[0]

        for g, i in others():
            @pl.when(g + i > 0)
            def _():
                value_copy(g, i, me * owners + block).start()

        value_got[me * owners + block] = value_out[here]

    @pl.loop(0, inner)
    def _(i):
        @pl.when(mine(i))
        def _():
            taps_copy(i, 0).wait_recv()

    relay_copy(parity).start()
    for n in range(5, 11):
        loads[n].wait()

    def local(which):
        for k in range(inner // 2):
            start = (2 * k + which) * width
            cols = pl.ds(pl.multiple_of(start, LANES), width)
            signal = signal_ref[:, cols]
            spectrum = dot(forward_ref[...], jnp.concatenate([signal, signal]))
            filters = jnp.concatenate([
                taps_buf[which, k], skip_ref[:, cols], jnp.zeros((7, width), F32),
            ])
            high, low = pieces(filters)
            response = dot(response_ref[...], jnp.concatenate([high, low, high]))
            s_re, s_im = spectrum[:rows], spectrum[rows:]
            r_re, r_im = response[:rows], response[rows:]
            product = jnp.concatenate([
                s_re * r_re - s_im * r_im, s_re * r_im + s_im * r_re,
            ])
            high, low = pieces(product)
            two = dot(inverse_ref[...], high)
            one = dot(inverse_ref[:rows], low)
            y_buf[:, cols] = two[:rows] + (two[rows:] + one)

    @pl.loop(0, 2)
    def _(step):
        @pl.when(step == 1)
        def _():
            relay_copy(1 - parity).wait_recv()

        local(jnp.where(step == 0, parity, 1 - parity))

    @pl.when(here == 0)
    def _():
        value_got[...] = jnp.zeros_like(value_got)

    @pl.loop(0, 2)
    def _(step):
        n = jnp.where(me < inner // 2, step, 1 - step)
        count = owners * inner // 2

        @pl.when(here > 0)
        def _():
            @pl.loop(0, count)
            def _(k):
                t = n * count + k

                @pl.when(jnp.logical_or(t // owners != me, t % owners != block))
                def _():
                    value_copy(0, 0, t).wait_recv()

        value = jnp.concatenate([value_got[n * count + k] for k in range(count)], axis=1)
        high, low = pieces(jnp.concatenate([value, jnp.zeros_like(value)]))
        carried = dot(carry_ref[...], jnp.concatenate([high, low, high]))
        gate = gating_ref[:, stretch(n)].astype(F32)
        out_buf[:, stretch(n)] = (gate * (y_buf[:, stretch(n)] + carried)).astype(BF16)
        out_copy(n).start()

    @pl.loop(0, inner)
    def _(i):
        @pl.when(mine(i))
        def _():
            taps_copy(me, i).wait_send()

    relay_copy(parity).wait_send()

    if owners == groups:
        for g, i in others():
            part_copy(g, i, here).wait_send()
    else:
        for r in order:
            for g in range(owners):
                @pl.when(jnp.logical_or(r > 0, block != g))
                def _():
                    part_copy(g, wrap(me + r, inner), here).wait_send()

    @pl.when(owns)
    def _():
        for g, i in others():
            @pl.when(g + i > 0)
            def _():
                value_copy(g, i, me * owners + block).wait_send()

    for n in range(2):
        out_copy(n).wait()


def per_device(signal, gating, decay_rate, residues, skip_gain):
    groups = lax.axis_size("outer")
    inner = lax.axis_size("inner")
    rows, channels = signal.shape
    width, modes = decay_rate.shape
    owners = max(1, min(groups, width // LANES))
    share = width // owners
    blocks = groups * inner
    dma = pltpu.SemaphoreType.DMA
    nodes, constants = tables(rows)
    arguments = (
        decay_rate.T, residues.T, signal, gating, skip_gain[None, :],
        *[jnp.asarray(c) for c in constants],
    )

    return pl.pallas_call(
        functools.partial(kernel, groups, inner, owners, modes, nodes),
        out_shape=jax.ShapeDtypeStruct((rows, channels), BF16),
        in_specs=[pl.BlockSpec(memory_space=pltpu.HBM)] * len(arguments),
        out_specs=pl.BlockSpec(memory_space=pltpu.HBM),
        scratch_shapes=[
            *[pltpu.VMEM(a.shape, a.dtype) for a in arguments],
            pltpu.VMEM((rows, channels), BF16),
            pltpu.VMEM((rows, channels), F32),
            pltpu.VMEM((NODES, modes, share), F32),
            pltpu.VMEM((modes, NODES, width), F32),
            pltpu.VMEM((NODES, width), F32),
            pltpu.VMEM((2, inner // 2, NODES, width), F32),
            pltpu.VMEM((owners * inner, NODES, share), F32),
            pltpu.VMEM((blocks, NODES, share), F32),
            pltpu.VMEM((blocks, modes, share), F32),
            pltpu.VMEM((blocks, NODES, share), F32),
            pltpu.VMEM((owners * inner, NODES, share), F32),
            pltpu.VMEM((modes, width), F32),
            dma((len(arguments),)), dma((2,)),
            dma((inner,)), dma((inner,)), dma(()), dma(()),
            dma((owners * inner,)), dma((blocks,)), dma((blocks,)), dma((owners * inner,)),
        ],
        compiler_params=pltpu.CompilerParams(
            collective_id=0, has_side_effects=True, vmem_limit_bytes=56 * 1024 * 1024
        ),
        name="modal_scan",
    )(*arguments)


def solution(mesh):
    return jax.shard_map(
        per_device,
        mesh=mesh,
        in_specs=(
            P(("outer", "inner"), None),
            P(("outer", "inner"), None),
            P("inner", None),
            P("inner", None),
            P(),
        ),
        out_specs=P(("outer", "inner"), None),
        check_vma=False,
    )
```

```python
import functools

import jax
import jax.numpy as jnp
import numpy as np
from jax import lax
from jax.experimental import pallas as pl
from jax.experimental.pallas import tpu as pltpu
from jax.sharding import PartitionSpec as P

MESH = pl.DeviceIdType.MESH
LANES = 128
F32 = jnp.float32
BF16 = jnp.bfloat16

MOST = 0.05
NODES = 8
NODES_S = (0.00578542, 0.05933078, 0.16499424, 0.31771443,
           0.50753127, 0.70895063, 0.88350275, 0.98635752)
NODES_R = (0.00681489, 0.06128461, 0.17012907, 0.34307065,
           0.48045442, 0.7017412, 0.88152977, 0.98619637)


def wrap(value, size):
    return lax.rem(value + size, size)


def one_minus_exp(z):
    series = jnp.ones_like(z)
    for n in range(12, 1, -1):
        series = 1.0 - series * z * (1.0 / n)
    return jnp.where(z < 0.5, z * series, 1.0 - jnp.exp(-z))


def eliminate(matrix, right):
    matrix, right = matrix.copy(), right.copy()
    size = len(matrix)
    for i in range(size):
        best = i + int(np.argmax(np.abs(matrix[i:, i])))
        matrix[[i, best]], right[[i, best]] = matrix[[best, i]], right[[best, i]]
        for k in range(i + 1, size):
            factor = matrix[k, i] / matrix[i, i]
            matrix[k] -= factor * matrix[i]
            right[k] -= factor * right[i]
    for i in range(size - 1, -1, -1):
        for k in range(i + 1, size):
            right[i] -= matrix[i, k] * right[k]
        right[i] /= matrix[i, i]
    return right


def split(array):
    high = array.astype(jnp.bfloat16)
    low = (array - high.astype(np.float64)).astype(jnp.bfloat16)
    return high, low


def tables(rows):
    assert rows <= 128
    s = np.arange(rows, dtype=np.float64)
    nodes = np.array(NODES_S) * (rows - 1)
    rates = np.array(NODES_R) * MOST
    cards = eliminate(np.exp(-rates[:, None] * nodes), np.exp(-rates[:, None] * s))
    angle = np.pi * (2.0 * s[:, None] + 1.0) / (2.0 * rows) * s[None, :]
    cos, sin = np.cos(angle), np.sin(angle)
    forward = np.concatenate([cos, -sin])
    inverse = np.concatenate([cos.T, -sin.T], axis=1) / rows
    taps = np.zeros((16, rows))
    taps[:NODES] = cards
    taps[NODES, 0] = 1.0
    response = forward @ taps.T
    ends = np.zeros((8, rows))
    ends[:NODES] = cards[:, ::-1]
    carry = np.zeros((rows, 16))
    carry[:, :NODES] = cards.T
    f_high, f_low = split(forward)
    r_high, r_low = split(response)
    i_high, i_low = split(inverse)
    e_high, e_low = split(ends)
    c_high, c_low = split(carry)
    node_rows = np.repeat(nodes[:, None], LANES, axis=1).astype(np.float32)
    return nodes, (
        np.concatenate([f_high, f_low], axis=1),
        np.concatenate([r_high, r_high, r_low], axis=1),
        np.concatenate([i_high, i_low]),
        np.concatenate([e_high, e_low]),
        np.concatenate([c_high, c_high, c_low], axis=1),
        node_rows,
    )


def pieces(value):
    high = value.astype(BF16)
    return high, (value - high.astype(F32)).astype(BF16)


def dot(a, b):
    return jnp.dot(a, b, preferred_element_type=F32)


def kernel(
    groups, inner, owners, modes, nodes,
    rate_hbm, residue_hbm, signal_hbm, gating_hbm, skip_hbm,
    forward_hbm, response_hbm, inverse_hbm, ends_hbm, carry_hbm, node_hbm, out_hbm,
    rate_ref, residue_ref, signal_ref, gating_ref, skip_ref,
    forward_ref, response_ref, inverse_ref, ends_ref, carry_ref, node_ref,
    out_buf, y_buf, phi_buf, wphi_buf, taps_own, taps_buf, part_out, part_got, state_buf,
    value_out, value_got, row_buf,
    load_sem, out_sem, taps_send, taps_recv, relay_send, relay_recv, part_send, part_recv,
    value_send, value_recv,
):
    me = lax.axis_index("inner")
    block = lax.axis_index("outer")
    half = lax.rem(block, 2)
    twin = block + 1 - 2 * half
    rows, channels = signal_ref.shape
    width = rate_ref.shape[1]
    share = width // owners
    blocks = groups * inner
    here = block * inner + me
    owns = block < owners
    own_cols = pl.ds(pl.multiple_of(lax.rem(block, owners) * share, LANES), share)

    def others(falling=False):
        for r in reversed(range(inner)) if falling else range(inner):
            for g in range(groups):
                if r or g:
                    yield wrap(block + g, groups), wrap(me + r, inner)

    barrier = pltpu.get_barrier_semaphore()
    for g, i in others():
        pl.semaphore_signal(
            barrier, inc=1, device_id={"outer": g, "inner": i}, device_id_type=MESH
        )

    loads = [
        pltpu.make_async_copy(source, target, load_sem.at[n])
        for n, (source, target) in enumerate((
            (rate_hbm, rate_ref), (residue_hbm, residue_ref), (node_hbm, node_ref),
            (ends_hbm, ends_ref), (signal_hbm, signal_ref),
            (forward_hbm, forward_ref), (response_hbm, response_ref),
            (inverse_hbm, inverse_ref), (skip_hbm, skip_ref), (carry_hbm, carry_ref),
            (gating_hbm, gating_ref),
        ))
    ]
    for load in loads:
        load.start()

    def remote(source, target, send, recv, device):
        return pltpu.make_async_remote_copy(
            src_ref=source, dst_ref=target, send_sem=send, recv_sem=recv,
            device_id=device, device_id_type=MESH,
        )

    def taps_copy(source, i):
        return remote(
            taps_own, taps_buf.at[source % 2, source // 2],
            taps_send.at[i], taps_recv.at[source], {"inner": i},
        )

    def relay_copy(parity):
        return remote(
            taps_buf.at[parity], taps_buf.at[parity],
            relay_send, relay_recv, {"outer": twin},
        )

    def part_copy(g, i, source):
        return remote(
            part_out.at[i * owners + g], part_got.at[source],
            part_send.at[i * owners + g], part_recv.at[source], {"outer": g, "inner": i},
        )

    def value_copy(g, i, source):
        return remote(
            value_out.at[g * inner + i], value_got.at[source],
            value_send.at[g * inner + i], value_recv.at[source], {"outer": g, "inner": i},
        )

    def stretch(n):
        size = channels // 2
        return pl.ds(pl.multiple_of(n * size, LANES), size)

    def out_copy(n):
        return pltpu.make_async_copy(
            out_buf.at[:, stretch(n)], out_hbm.at[:, stretch(n)], out_sem.at[n]
        )

    for n in range(3):
        loads[n].wait()
    own_rate = rate_ref[:, own_cols]
    for j in range(NODES):
        phi_buf[j] = jnp.exp(own_rate * (-float(nodes[j])))
    row_buf[...] = residue_ref[...] * jnp.sqrt(one_minus_exp(2.0 * rate_ref[...]))
    node_col = jnp.concatenate([node_ref[...]] * (width // LANES), axis=1)
    taps = jnp.zeros((NODES, width), F32)
    for m in range(modes):
        value = row_buf[m : m + 1, :] * jnp.exp(-(rate_ref[m : m + 1, :] * node_col))
        wphi_buf[m] = value
        taps = taps + value
    taps_own[...] = taps
    parity = lax.rem(half + me, 2)

    @pl.when(half == 0)
    def _():
        taps_buf[parity, me // 2] = taps

    loads[3].wait()
    loads[4].wait()
    for n in range(2):
        both = dot(ends_ref[...], signal_ref[:, n * channels // 2 : (n + 1) * channels // 2])
        part = both[:NODES] + both[NODES:]
        for k in range(owners * inner // 2):
            part_out[n * owners * inner // 2 + k] = part[:, k * share : (k + 1) * share]

    pl.semaphore_wait(barrier, blocks - 1)

    if owners == groups:
        for g, i in others(falling=True):
            part_copy(g, i, here).start()
    else:
        for r in range(inner):
            for g in range(owners):
                @pl.when(jnp.logical_or(r > 0, block != g))
                def _():
                    part_copy(g, wrap(me + r, inner), here).start()

    def mine(i):
        return jnp.logical_and(lax.rem(i + me, 2) == half, i != me)

    @pl.loop(0, inner)
    def _(i):
        @pl.when(mine(i))
        def _():
            taps_copy(me, i).start()

    @pl.when(owns)
    def _():
        part_got[here] = part_out[me * owners + block]
        own_rate = rate_ref[:, own_cols]
        decay_block = jnp.exp(own_rate * (-float(rows)))
        decay_one = jnp.exp(-own_rate)

        def advance(p, run):
            @pl.when(p != here)
            def _():
                part_copy(0, 0, p).wait_recv()

            state_buf[p] = decay_one * run
            ends = [phi_buf[j] * part_got[p, j : j + 1, :] for j in range(NODES)]
            while len(ends) > 1:
                ends = [a + b for a, b in zip(ends[::2], ends[1::2])]
            return decay_block * run + ends[0]

        lax.fori_loop(0, blocks, advance, jnp.zeros((modes, share), F32), unroll=4)

        for i in range(inner):
            for g in range(groups):
                p = g * inner + i
                terms = [
                    wphi_buf[m, :, own_cols] * state_buf[p, m : m + 1, :]
                    for m in range(modes)
                ]
                while len(terms) > 1:
                    terms = [a + b for a, b in zip(terms[::2], terms[1::2])]
                value_out[p] = terms[0]

            for g in range(groups):
                if g + i > 0:
                    @pl.when(here != g * inner + i)
                    def _():
                        value_copy(g, i, me * owners + block).start()

        value_got[me * owners + block] = value_out[here]

    @pl.loop(0, inner)
    def _(i):
        @pl.when(mine(i))
        def _():
            taps_copy(i, 0).wait_recv()

    relay_copy(parity).start()
    for n in range(5, 11):
        loads[n].wait()

    def local(which):
        for k in range(inner // 2):
            start = (2 * k + which) * width
            cols = pl.ds(pl.multiple_of(start, LANES), width)
            signal = signal_ref[:, cols]
            spectrum = dot(forward_ref[...], jnp.concatenate([signal, signal]))
            filters = jnp.concatenate([
                taps_buf[which, k], skip_ref[:, cols], jnp.zeros((7, width), F32),
            ])
            high, low = pieces(filters)
            response = dot(response_ref[...], jnp.concatenate([high, low, high]))
            s_re, s_im = spectrum[:rows], spectrum[rows:]
            r_re, r_im = response[:rows], response[rows:]
            product = jnp.concatenate([
                s_re * r_re - s_im * r_im, s_re * r_im + s_im * r_re,
            ])
            high, low = pieces(product)
            two = dot(inverse_ref[...], high)
            one = dot(inverse_ref[:rows], low)
            y_buf[:, cols] = two[:rows] + (two[rows:] + one)

    @pl.loop(0, 2)
    def _(step):
        @pl.when(step == 1)
        def _():
            relay_copy(1 - parity).wait_recv()

        local(jnp.where(step == 0, parity, 1 - parity))

    @pl.when(here == 0)
    def _():
        value_got[...] = jnp.zeros_like(value_got)

    @pl.loop(0, 2)
    def _(step):
        n = jnp.where(me < inner // 2, step, 1 - step)
        count = owners * inner // 2

        @pl.when(here > 0)
        def _():
            @pl.loop(0, count)
            def _(k):
                t = n * count + k

                @pl.when(jnp.logical_or(t // owners != me, t % owners != block))
                def _():
                    value_copy(0, 0, t).wait_recv()

        value = jnp.concatenate([value_got[n * count + k] for k in range(count)], axis=1)
        high, low = pieces(jnp.concatenate([value, jnp.zeros_like(value)]))
        carried = dot(carry_ref[...], jnp.concatenate([high, low, high]))
        gate = gating_ref[:, stretch(n)].astype(F32)
        out_buf[:, stretch(n)] = (gate * (y_buf[:, stretch(n)] + carried)).astype(BF16)
        out_copy(n).start()

    @pl.loop(0, inner)
    def _(i):
        @pl.when(mine(i))
        def _():
            taps_copy(me, i).wait_send()

    relay_copy(parity).wait_send()

    if owners == groups:
        for g, i in others():
            part_copy(g, i, here).wait_send()
    else:
        for r in range(inner):
            for g in range(owners):
                @pl.when(jnp.logical_or(r > 0, block != g))
                def _():
                    part_copy(g, wrap(me + r, inner), here).wait_send()

    @pl.when(owns)
    def _():
        @pl.loop(1, blocks)
        def _(p):
            @pl.when(p != here)
            def _():
                value_copy(p // inner, p % inner, 0).wait_send()

    for n in range(2):
        out_copy(n).wait()


def per_device(signal, gating, decay_rate, residues, skip_gain):
    groups = lax.axis_size("outer")
    inner = lax.axis_size("inner")
    rows, channels = signal.shape
    width, modes = decay_rate.shape
    owners = max(1, min(groups, width // LANES))
    share = width // owners
    blocks = groups * inner
    dma = pltpu.SemaphoreType.DMA
    nodes, constants = tables(rows)
    arguments = (
        decay_rate.T, residues.T, signal, gating, skip_gain[None, :],
        *[jnp.asarray(c) for c in constants],
    )

    return pl.pallas_call(
        functools.partial(kernel, groups, inner, owners, modes, nodes),
        out_shape=jax.ShapeDtypeStruct((rows, channels), BF16),
        in_specs=[pl.BlockSpec(memory_space=pltpu.HBM)] * len(arguments),
        out_specs=pl.BlockSpec(memory_space=pltpu.HBM),
        scratch_shapes=[
            *[pltpu.VMEM(a.shape, a.dtype) for a in arguments],
            pltpu.VMEM((rows, channels), BF16),
            pltpu.VMEM((rows, channels), F32),
            pltpu.VMEM((NODES, modes, share), F32),
            pltpu.VMEM((modes, NODES, width), F32),
            pltpu.VMEM((NODES, width), F32),
            pltpu.VMEM((2, inner // 2, NODES, width), F32),
            pltpu.VMEM((owners * inner, NODES, share), F32),
            pltpu.VMEM((blocks, NODES, share), F32),
            pltpu.VMEM((blocks, modes, share), F32),
            pltpu.VMEM((blocks, NODES, share), F32),
            pltpu.VMEM((owners * inner, NODES, share), F32),
            pltpu.VMEM((modes, width), F32),
            dma((len(arguments),)), dma((2,)),
            dma((inner,)), dma((inner,)), dma(()), dma(()),
            dma((owners * inner,)), dma((blocks,)), dma((blocks,)), dma((owners * inner,)),
        ],
        compiler_params=pltpu.CompilerParams(
            collective_id=0, has_side_effects=True, vmem_limit_bytes=56 * 1024 * 1024
        ),
        name="modal_scan",
    )(*arguments)


def solution(mesh):
    return jax.shard_map(
        per_device,
        mesh=mesh,
        in_specs=(
            P(("outer", "inner"), None),
            P(("outer", "inner"), None),
            P("inner", None),
            P("inner", None),
            P(),
        ),
        out_specs=P(("outer", "inner"), None),
        check_vma=False,
    )
```

```python
import functools

import jax
import jax.numpy as jnp
import numpy as np
from jax import lax
from jax.experimental import pallas as pl
from jax.experimental.pallas import tpu as pltpu
from jax.sharding import PartitionSpec as P

MESH = pl.DeviceIdType.MESH
LANES = 128
F32 = jnp.float32
BF16 = jnp.bfloat16

MOST = 0.05
NODES = 8
NODES_S = (0.00578542, 0.05933078, 0.16499424, 0.31771443,
           0.50753127, 0.70895063, 0.88350275, 0.98635752)
NODES_R = (0.00681489, 0.06128461, 0.17012907, 0.34307065,
           0.48045442, 0.7017412, 0.88152977, 0.98619637)


def wrap(value, size):
    return lax.rem(value + size, size)


def one_minus_exp(z):
    series = jnp.ones_like(z)
    for n in range(12, 1, -1):
        series = 1.0 - series * z * (1.0 / n)
    return jnp.where(z < 0.5, z * series, 1.0 - jnp.exp(-z))


def eliminate(matrix, right):
    matrix, right = matrix.copy(), right.copy()
    size = len(matrix)
    for i in range(size):
        best = i + int(np.argmax(np.abs(matrix[i:, i])))
        matrix[[i, best]], right[[i, best]] = matrix[[best, i]], right[[best, i]]
        for k in range(i + 1, size):
            factor = matrix[k, i] / matrix[i, i]
            matrix[k] -= factor * matrix[i]
            right[k] -= factor * right[i]
    for i in range(size - 1, -1, -1):
        for k in range(i + 1, size):
            right[i] -= matrix[i, k] * right[k]
        right[i] /= matrix[i, i]
    return right


def split(array):
    high = array.astype(jnp.bfloat16)
    low = (array - high.astype(np.float64)).astype(jnp.bfloat16)
    return high, low


def tables(rows):
    assert rows <= 128
    s = np.arange(rows, dtype=np.float64)
    nodes = np.array(NODES_S) * (rows - 1)
    rates = np.array(NODES_R) * MOST
    cards = eliminate(np.exp(-rates[:, None] * nodes), np.exp(-rates[:, None] * s))
    angle = np.pi * (2.0 * s[:, None] + 1.0) / (2.0 * rows) * s[None, :]
    cos, sin = np.cos(angle), np.sin(angle)
    forward = np.concatenate([cos, -sin])
    inverse = np.concatenate([cos.T, -sin.T], axis=1) / rows
    taps = np.zeros((16, rows))
    taps[:NODES] = cards
    taps[NODES, 0] = 1.0
    response = forward @ taps.T
    ends = np.zeros((8, rows))
    ends[:NODES] = cards[:, ::-1]
    carry = np.zeros((rows, 16))
    carry[:, :NODES] = cards.T
    f_high, f_low = split(forward)
    r_high, r_low = split(response)
    i_high, i_low = split(inverse)
    e_high, e_low = split(ends)
    c_high, c_low = split(carry)
    node_rows = np.repeat(nodes[:, None], LANES, axis=1).astype(np.float32)
    return nodes, (
        np.concatenate([f_high, f_low], axis=1),
        np.concatenate([r_high, r_high, r_low], axis=1),
        np.concatenate([i_high, i_low]),
        np.concatenate([e_high, e_low]),
        np.concatenate([c_high, c_high, c_low], axis=1),
        node_rows,
    )


def pieces(value):
    high = value.astype(BF16)
    return high, (value - high.astype(F32)).astype(BF16)


def dot(a, b):
    return jnp.dot(a, b, preferred_element_type=F32)


def kernel(
    groups, inner, owners, modes, nodes,
    rate_hbm, residue_hbm, signal_hbm, gating_hbm, skip_hbm,
    forward_hbm, response_hbm, inverse_hbm, ends_hbm, carry_hbm, node_hbm, out_ref,
    rate_ref, residue_ref, signal_ref, gating_ref, skip_ref,
    forward_ref, response_ref, inverse_ref, ends_ref, carry_ref, node_ref,
    y_buf, phi_buf, wphi_buf, taps_own, taps_buf, part_out, part_got, state_buf,
    value_out, value_got, row_buf,
    load_sem, taps_send, taps_recv, relay_send, relay_recv, part_send, part_recv,
    value_send, value_recv,
):
    me = lax.axis_index("inner")
    block = lax.axis_index("outer")
    half = lax.rem(block, 2)
    twin = block + 1 - 2 * half
    rows, channels = signal_ref.shape
    width = rate_ref.shape[1]
    share = width // owners
    blocks = groups * inner
    here = block * inner + me
    owns = block < owners
    own_cols = pl.ds(pl.multiple_of(lax.rem(block, owners) * share, LANES), share)

    def others(falling=False):
        for r in reversed(range(inner)) if falling else range(inner):
            for g in range(groups):
                if r or g:
                    yield wrap(block + g, groups), wrap(me + r, inner)

    barrier = pltpu.get_barrier_semaphore()
    for g, i in others():
        pl.semaphore_signal(
            barrier, inc=1, device_id={"outer": g, "inner": i}, device_id_type=MESH
        )

    loads = [
        pltpu.make_async_copy(source, target, load_sem.at[n])
        for n, (source, target) in enumerate((
            (rate_hbm, rate_ref), (residue_hbm, residue_ref), (node_hbm, node_ref),
            (ends_hbm, ends_ref), (signal_hbm, signal_ref),
            (forward_hbm, forward_ref), (response_hbm, response_ref),
            (inverse_hbm, inverse_ref), (skip_hbm, skip_ref), (carry_hbm, carry_ref),
            (gating_hbm, gating_ref),
        ))
    ]
    for load in loads:
        load.start()

    def remote(source, target, send, recv, device):
        return pltpu.make_async_remote_copy(
            src_ref=source, dst_ref=target, send_sem=send, recv_sem=recv,
            device_id=device, device_id_type=MESH,
        )

    def taps_copy(source, i):
        return remote(
            taps_own, taps_buf.at[source % 2, source // 2],
            taps_send.at[i], taps_recv.at[source], {"inner": i},
        )

    def relay_copy(parity):
        return remote(
            taps_buf.at[parity], taps_buf.at[parity],
            relay_send, relay_recv, {"outer": twin},
        )

    def part_copy(g, i, source):
        return remote(
            part_out.at[i * owners + g], part_got.at[source],
            part_send.at[i * owners + g], part_recv.at[source], {"outer": g, "inner": i},
        )

    def value_copy(g, i, source):
        return remote(
            value_out.at[g * inner + i], value_got.at[source],
            value_send.at[g * inner + i], value_recv.at[source], {"outer": g, "inner": i},
        )

    def stretch(n):
        size = channels // 2
        return pl.ds(pl.multiple_of(n * size, LANES), size)

    for n in range(3):
        loads[n].wait()
    own_rate = rate_ref[:, own_cols]
    for j in range(NODES):
        phi_buf[j] = jnp.exp(own_rate * (-float(nodes[j])))
    row_buf[...] = residue_ref[...] * jnp.sqrt(one_minus_exp(2.0 * rate_ref[...]))
    node_col = jnp.concatenate([node_ref[...]] * (width // LANES), axis=1)
    taps = jnp.zeros((NODES, width), F32)
    for m in range(modes):
        value = row_buf[m : m + 1, :] * jnp.exp(-(rate_ref[m : m + 1, :] * node_col))
        wphi_buf[m] = value
        taps = taps + value
    taps_own[...] = taps
    parity = lax.rem(half + me, 2)

    @pl.when(half == 0)
    def _():
        taps_buf[parity, me // 2] = taps

    loads[3].wait()
    loads[4].wait()
    for n in range(2):
        both = dot(ends_ref[...], signal_ref[:, n * channels // 2 : (n + 1) * channels // 2])
        part = both[:NODES] + both[NODES:]
        for k in range(owners * inner // 2):
            part_out[n * owners * inner // 2 + k] = part[:, k * share : (k + 1) * share]

    pl.semaphore_wait(barrier, blocks - 1)

    if owners == groups:
        for g, i in others(falling=True):
            part_copy(g, i, here).start()
    else:
        for r in range(inner):
            for g in range(owners):
                @pl.when(jnp.logical_or(r > 0, block != g))
                def _():
                    part_copy(g, wrap(me + r, inner), here).start()

    def mine(i):
        return jnp.logical_and(lax.rem(i + me, 2) == half, i != me)

    @pl.loop(0, inner)
    def _(i):
        @pl.when(mine(i))
        def _():
            taps_copy(me, i).start()

    @pl.when(owns)
    def _():
        part_got[here] = part_out[me * owners + block]
        own_rate = rate_ref[:, own_cols]
        decay_block = jnp.exp(own_rate * (-float(rows)))
        decay_one = jnp.exp(-own_rate)

        def advance(p, run):
            @pl.when(p != here)
            def _():
                part_copy(0, 0, p).wait_recv()

            state_buf[p] = decay_one * run
            ends = [phi_buf[j] * part_got[p, j : j + 1, :] for j in range(NODES)]
            while len(ends) > 1:
                ends = [a + b for a, b in zip(ends[::2], ends[1::2])]
            return decay_block * run + ends[0]

        lax.fori_loop(0, blocks, advance, jnp.zeros((modes, share), F32), unroll=4)

        for i in range(inner):
            for g in range(groups):
                p = g * inner + i
                terms = [
                    wphi_buf[m, :, own_cols] * state_buf[p, m : m + 1, :]
                    for m in range(modes)
                ]
                while len(terms) > 1:
                    terms = [a + b for a, b in zip(terms[::2], terms[1::2])]
                value_out[p] = terms[0]

            for g in range(groups):
                if g + i > 0:
                    @pl.when(here != g * inner + i)
                    def _():
                        value_copy(g, i, me * owners + block).start()

        value_got[me * owners + block] = value_out[here]

    @pl.loop(0, inner)
    def _(i):
        @pl.when(mine(i))
        def _():
            taps_copy(i, 0).wait_recv()

    relay_copy(parity).start()
    for n in range(5, 11):
        loads[n].wait()

    def local(which):
        for k in range(inner // 2):
            start = (2 * k + which) * width
            cols = pl.ds(pl.multiple_of(start, LANES), width)
            signal = signal_ref[:, cols]
            spectrum = dot(forward_ref[...], jnp.concatenate([signal, signal]))
            filters = jnp.concatenate([
                taps_buf[which, k], skip_ref[:, cols], jnp.zeros((7, width), F32),
            ])
            high, low = pieces(filters)
            response = dot(response_ref[...], jnp.concatenate([high, low, high]))
            s_re, s_im = spectrum[:rows], spectrum[rows:]
            r_re, r_im = response[:rows], response[rows:]
            product = jnp.concatenate([
                s_re * r_re - s_im * r_im, s_re * r_im + s_im * r_re,
            ])
            high, low = pieces(product)
            two = dot(inverse_ref[...], high)
            one = dot(inverse_ref[:rows], low)
            y_buf[:, cols] = two[:rows] + (two[rows:] + one)

    @pl.loop(0, 2)
    def _(step):
        @pl.when(step == 1)
        def _():
            relay_copy(1 - parity).wait_recv()

        local(jnp.where(step == 0, parity, 1 - parity))

    @pl.when(here == 0)
    def _():
        value_got[...] = jnp.zeros_like(value_got)

    @pl.loop(0, 2)
    def _(step):
        n = jnp.where(me < inner // 2, step, 1 - step)
        count = owners * inner // 2

        @pl.when(here > 0)
        def _():
            @pl.loop(0, count)
            def _(k):
                t = n * count + k

                @pl.when(jnp.logical_or(t // owners != me, t % owners != block))
                def _():
                    value_copy(0, 0, t).wait_recv()

        value = jnp.concatenate([value_got[n * count + k] for k in range(count)], axis=1)
        high, low = pieces(jnp.concatenate([value, jnp.zeros_like(value)]))
        carried = dot(carry_ref[...], jnp.concatenate([high, low, high]))
        gate = gating_ref[:, stretch(n)].astype(F32)
        out_ref[:, stretch(n)] = (gate * (y_buf[:, stretch(n)] + carried)).astype(BF16)

    @pl.loop(0, inner)
    def _(i):
        @pl.when(mine(i))
        def _():
            taps_copy(me, i).wait_send()

    relay_copy(parity).wait_send()

    if owners == groups:
        for g, i in others():
            part_copy(g, i, here).wait_send()
    else:
        for r in range(inner):
            for g in range(owners):
                @pl.when(jnp.logical_or(r > 0, block != g))
                def _():
                    part_copy(g, wrap(me + r, inner), here).wait_send()

    @pl.when(owns)
    def _():
        @pl.loop(1, blocks)
        def _(p):
            @pl.when(p != here)
            def _():
                value_copy(p // inner, p % inner, 0).wait_send()


def per_device(signal, gating, decay_rate, residues, skip_gain):
    groups = lax.axis_size("outer")
    inner = lax.axis_size("inner")
    rows, channels = signal.shape
    width, modes = decay_rate.shape
    owners = max(1, min(groups, width // LANES))
    share = width // owners
    blocks = groups * inner
    dma = pltpu.SemaphoreType.DMA
    nodes, constants = tables(rows)
    arguments = (
        decay_rate.T, residues.T, signal, gating, skip_gain[None, :],
        *[jnp.asarray(c) for c in constants],
    )

    return pl.pallas_call(
        functools.partial(kernel, groups, inner, owners, modes, nodes),
        out_shape=jax.ShapeDtypeStruct((rows, channels), BF16),
        in_specs=[pl.BlockSpec(memory_space=pltpu.HBM)] * len(arguments),
        out_specs=pl.BlockSpec(memory_space=pltpu.VMEM),
        scratch_shapes=[
            *[pltpu.VMEM(a.shape, a.dtype) for a in arguments],
            pltpu.VMEM((rows, channels), F32),
            pltpu.VMEM((NODES, modes, share), F32),
            pltpu.VMEM((modes, NODES, width), F32),
            pltpu.VMEM((NODES, width), F32),
            pltpu.VMEM((2, inner // 2, NODES, width), F32),
            pltpu.VMEM((owners * inner, NODES, share), F32),
            pltpu.VMEM((blocks, NODES, share), F32),
            pltpu.VMEM((blocks, modes, share), F32),
            pltpu.VMEM((blocks, NODES, share), F32),
            pltpu.VMEM((owners * inner, NODES, share), F32),
            pltpu.VMEM((modes, width), F32),
            dma((len(arguments),)),
            dma((inner,)), dma((inner,)), dma(()), dma(()),
            dma((owners * inner,)), dma((blocks,)), dma((blocks,)), dma((owners * inner,)),
        ],
        compiler_params=pltpu.CompilerParams(
            collective_id=0, has_side_effects=True, vmem_limit_bytes=24 << 20
        ),
        name="modal_scan",
    )(*[pltpu.with_memory_space_constraint(a, pltpu.HBM) for a in arguments])


def solution(mesh):
    return jax.shard_map(
        per_device,
        mesh=mesh,
        in_specs=(
            P(("outer", "inner"), None),
            P(("outer", "inner"), None),
            P("inner", None),
            P("inner", None),
            P(),
        ),
        out_specs=P(("outer", "inner"), None),
        check_vma=False,
    )
```

```python
import functools

import jax
import jax.numpy as jnp
import numpy as np
from jax import lax
from jax.experimental import pallas as pl
from jax.experimental.pallas import tpu as pltpu
from jax.sharding import PartitionSpec as P

MESH = pl.DeviceIdType.MESH
LANES = 128
F32 = jnp.float32
BF16 = jnp.bfloat16

MOST = 0.05
NODES = 8
NODES_S = (0.00578542, 0.05933078, 0.16499424, 0.31771443,
           0.50753127, 0.70895063, 0.88350275, 0.98635752)
NODES_R = (0.00681489, 0.06128461, 0.17012907, 0.34307065,
           0.48045442, 0.7017412, 0.88152977, 0.98619637)


def wrap(value, size):
    return lax.rem(value + size, size)


def one_minus_exp(z):
    series = jnp.ones_like(z)
    for n in range(12, 1, -1):
        series = 1.0 - series * z * (1.0 / n)
    return jnp.where(z < 0.5, z * series, 1.0 - jnp.exp(-z))


def eliminate(matrix, right):
    matrix, right = matrix.copy(), right.copy()
    size = len(matrix)
    for i in range(size):
        best = i + int(np.argmax(np.abs(matrix[i:, i])))
        matrix[[i, best]], right[[i, best]] = matrix[[best, i]], right[[best, i]]
        for k in range(i + 1, size):
            factor = matrix[k, i] / matrix[i, i]
            matrix[k] -= factor * matrix[i]
            right[k] -= factor * right[i]
    for i in range(size - 1, -1, -1):
        for k in range(i + 1, size):
            right[i] -= matrix[i, k] * right[k]
        right[i] /= matrix[i, i]
    return right


def split(array):
    high = array.astype(jnp.bfloat16)
    low = (array - high.astype(np.float64)).astype(jnp.bfloat16)
    return high, low


def tables(rows):
    assert rows <= 128
    s = np.arange(rows, dtype=np.float64)
    nodes = np.array(NODES_S) * (rows - 1)
    rates = np.array(NODES_R) * MOST
    cards = eliminate(np.exp(-rates[:, None] * nodes), np.exp(-rates[:, None] * s))
    angle = np.pi * (2.0 * s[:, None] + 1.0) / (2.0 * rows) * s[None, :]
    cos, sin = np.cos(angle), np.sin(angle)
    forward = np.concatenate([cos, -sin])
    inverse = np.concatenate([cos.T, -sin.T], axis=1) / rows
    taps = np.zeros((16, rows))
    taps[:NODES] = cards
    taps[NODES, 0] = 1.0
    response = forward @ taps.T
    ends = np.zeros((8, rows))
    ends[:NODES] = cards[:, ::-1]
    carry = np.zeros((rows, 16))
    carry[:, :NODES] = cards.T
    f_high, f_low = split(forward)
    r_high, r_low = split(response)
    i_high, i_low = split(inverse)
    e_high, e_low = split(ends)
    c_high, c_low = split(carry)
    node_rows = np.repeat(nodes[:, None], LANES, axis=1).astype(np.float32)
    return nodes, (
        np.concatenate([f_high, f_low], axis=1),
        np.concatenate([r_high, r_high, r_low], axis=1),
        np.concatenate([i_high, i_low]),
        np.concatenate([e_high, e_low]),
        np.concatenate([c_high, c_high, c_low], axis=1),
        node_rows,
    )


def pieces(value):
    high = value.astype(BF16)
    return high, (value - high.astype(F32)).astype(BF16)


def dot(a, b):
    return jnp.dot(a, b, preferred_element_type=F32)


def kernel(
    groups, inner, owners, modes, nodes,
    rate_hbm, residue_hbm, signal_hbm, gating_hbm, skip_hbm,
    forward_hbm, response_hbm, inverse_hbm, ends_hbm, carry_hbm, node_hbm, out_ref,
    rate_ref, residue_ref, signal_ref, gating_ref, skip_ref,
    forward_ref, response_ref, inverse_ref, ends_ref, carry_ref, node_ref,
    y_buf, phi_buf, wphi_buf, taps_own, taps_buf, part_out, part_got, state_buf,
    value_out, value_got, row_buf, rates_own, rates_got, both_buf,
    load_sem, taps_send, taps_recv, relay_send, relay_recv, part_send, part_recv,
    value_send, value_recv, rates_send, rates_recv,
):
    me = lax.axis_index("inner")
    block = lax.axis_index("outer")
    half = lax.rem(block, 2)
    twin = block + 1 - 2 * half
    rows, channels = signal_ref.shape
    width = rate_ref.shape[1]
    share = width // owners
    blocks = groups * inner
    quarter = inner // 4
    count = owners * quarter
    here = block * inner + me
    first = me < inner // 2
    own_cols = pl.ds(pl.multiple_of(lax.rem(block, owners) * share, LANES), share)

    def owner(g, i):
        return jnp.logical_and(g < owners, jnp.logical_and(i >= quarter, i < 3 * quarter))

    owns = owner(block, me)
    place = (me - quarter) * owners + block

    def others():
        for r in range(inner):
            for g in range(groups):
                if r or g:
                    yield wrap(block + g, groups), wrap(me + r, inner), g == 0

    barrier = pltpu.get_barrier_semaphore()
    greeted = jnp.int32(0)
    for g, i, together in others():
        meets = jnp.logical_or(jnp.logical_or(owns, owner(g, i)), jnp.logical_or(
            together, jnp.logical_and(g == twin, i == me)
        ))
        greeted = greeted + meets.astype(jnp.int32)

        @pl.when(meets)
        def _():
            pl.semaphore_signal(
                barrier, inc=1, device_id={"outer": g, "inner": i}, device_id_type=MESH
            )

    loads = [
        pltpu.make_async_copy(source, target, load_sem.at[n])
        for n, (source, target) in enumerate((
            (rate_hbm, rate_ref), (residue_hbm, residue_ref), (node_hbm, node_ref),
            (ends_hbm, ends_ref), (signal_hbm, signal_ref),
            (forward_hbm, forward_ref), (response_hbm, response_ref),
            (inverse_hbm, inverse_ref), (skip_hbm, skip_ref), (carry_hbm, carry_ref),
            (gating_hbm, gating_ref),
        ))
    ]
    for load in loads:
        load.start()

    def remote(source, target, send, recv, device):
        return pltpu.make_async_remote_copy(
            src_ref=source, dst_ref=target, send_sem=send, recv_sem=recv,
            device_id=device, device_id_type=MESH,
        )

    def taps_copy(source, i):
        return remote(
            taps_own, taps_buf.at[source % 2, source // 2],
            taps_send.at[i], taps_recv.at[source], {"inner": i},
        )

    def relay_copy(parity):
        return remote(
            taps_buf.at[parity], taps_buf.at[parity],
            relay_send, relay_recv, {"outer": twin},
        )

    def rates_copy():
        i = jnp.where(me < quarter, me + quarter, me - quarter)
        return remote(rates_own, rates_got, rates_send, rates_recv, {"inner": i})

    def part_copy(k, source):
        return remote(
            part_out.at[k], part_got.at[source], part_send.at[k], part_recv.at[source],
            {"outer": k % owners, "inner": quarter + k // owners},
        )

    def value_copy(target, k):
        return remote(
            value_out.at[target], value_got.at[k], value_send.at[target], value_recv.at[k],
            {"outer": target // inner, "inner": target % inner},
        )

    def stretch(n):
        size = channels // 2
        return pl.ds(pl.multiple_of(n * size, LANES), size)

    for n in range(3):
        loads[n].wait()
    rates_own[0] = rate_ref[:, own_cols]
    row_buf[...] = residue_ref[...] * jnp.sqrt(one_minus_exp(2.0 * rate_ref[...]))
    rates_own[1] = row_buf[:, own_cols]
    node_col = jnp.concatenate([node_ref[...]] * (width // LANES), axis=1)
    taps = jnp.zeros((NODES, width), F32)
    for m in range(modes):
        taps = taps + row_buf[m : m + 1, :] * jnp.exp(
            -(rate_ref[m : m + 1, :] * node_col)
        )
    taps_own[...] = taps
    parity = lax.rem(half + me, 2)

    @pl.when(half == 0)
    def _():
        taps_buf[parity, me // 2] = taps

    loads[3].wait()
    loads[4].wait()
    for n in range(2):
        both = dot(ends_ref[...], signal_ref[:, n * channels // 2 : (n + 1) * channels // 2])
        part = both[:NODES] + both[NODES:]
        for k in range(count):
            part_out[n * count + k] = jnp.concatenate([
                part[:, k * share : (k + 1) * share],
                part[:, (count + k) * share : (count + k + 1) * share],
            ], axis=1)

    pl.semaphore_wait(barrier, greeted)
    gives = jnp.logical_and(block < owners, jnp.logical_not(owns))

    @pl.when(gives)
    def _():
        rates_copy().start()

    def each_owner(act):
        for k in range(2 * count):
            @pl.when(jnp.logical_or(jnp.logical_not(owns), place != k))
            def _():
                act(k)

    each_owner(lambda k: part_copy(k, here).start())

    def mine(i):
        return jnp.logical_and(lax.rem(i + me, 2) == half, i != me)

    @pl.loop(0, inner)
    def _(i):
        @pl.when(mine(i))
        def _():
            taps_copy(me, i).start()

    @pl.when(owns)
    def _():
        for k in range(2 * count):
            @pl.when(place == k)
            def _():
                part_got[here] = part_out[k]

        rates_copy().wait_recv()
        for n in range(2):
            got, own = rates_got[n], rates_own[n]
            both_buf[n] = jnp.concatenate(
                [jnp.where(first, got, own), jnp.where(first, own, got)], axis=1
            )
        rate = both_buf[0]
        for j in range(NODES):
            phi_buf[j] = jnp.exp(rate * (-float(nodes[j])))
        node_col = jnp.concatenate([node_ref[...]] * (2 * share // LANES), axis=1)
        for m in range(modes):
            wphi_buf[m] = both_buf[1, m : m + 1, :] * jnp.exp(
                -(both_buf[0, m : m + 1, :] * node_col)
            )
        decay_block = jnp.exp(rate * (-float(rows)))
        decay_one = jnp.exp(-rate)

        def advance(p, run):
            @pl.when(p != here)
            def _():
                part_copy(0, p).wait_recv()

            state_buf[p] = decay_one * run
            ends = [phi_buf[j] * part_got[p, j : j + 1, :] for j in range(NODES)]
            while len(ends) > 1:
                ends = [a + b for a, b in zip(ends[::2], ends[1::2])]
            return decay_block * run + ends[0]

        lax.fori_loop(0, blocks, advance, jnp.zeros((modes, 2 * share), F32), unroll=4)

        for i in range(inner):
            for g in range(groups):
                p = g * inner + i
                terms = [
                    wphi_buf[m] * state_buf[p, m : m + 1, :] for m in range(modes)
                ]
                while len(terms) > 1:
                    terms = [a + b for a, b in zip(terms[::2], terms[1::2])]
                value_out[p] = terms[0]

            for g in range(groups):
                if g + i > 0:
                    @pl.when(here != g * inner + i)
                    def _():
                        value_copy(g * inner + i, place).start()

        for k in range(2 * count):
            @pl.when(place == k)
            def _():
                value_got[k] = value_out[here]

    @pl.loop(0, inner)
    def _(i):
        @pl.when(mine(i))
        def _():
            taps_copy(i, 0).wait_recv()

    relay_copy(parity).start()
    for n in range(5, 11):
        loads[n].wait()

    def local(which):
        for k in range(inner // 2):
            start = (2 * k + which) * width
            cols = pl.ds(pl.multiple_of(start, LANES), width)
            signal = signal_ref[:, cols]
            spectrum = dot(forward_ref[...], jnp.concatenate([signal, signal]))
            filters = jnp.concatenate([
                taps_buf[which, k], skip_ref[:, cols], jnp.zeros((7, width), F32),
            ])
            high, low = pieces(filters)
            response = dot(response_ref[...], jnp.concatenate([high, low, high]))
            s_re, s_im = spectrum[:rows], spectrum[rows:]
            r_re, r_im = response[:rows], response[rows:]
            product = jnp.concatenate([
                s_re * r_re - s_im * r_im, s_re * r_im + s_im * r_re,
            ])
            high, low = pieces(product)
            two = dot(inverse_ref[...], high)
            one = dot(inverse_ref[:rows], low)
            y_buf[:, cols] = two[:rows] + (two[rows:] + one)

    @pl.loop(0, 2)
    def _(step):
        @pl.when(step == 1)
        def _():
            relay_copy(1 - parity).wait_recv()

        local(jnp.where(step == 0, parity, 1 - parity))

    @pl.when(here == 0)
    def _():
        value_got[...] = jnp.zeros_like(value_got)

    @pl.loop(0, 2)
    def _(step):
        n = jnp.where(first, step, 1 - step)

        @pl.when(here > 0)
        def _():
            @pl.loop(n * count, (n + 1) * count)
            def _(k):
                @pl.when(jnp.logical_or(jnp.logical_not(owns), place != k))
                def _():
                    value_copy(0, k).wait_recv()

        value = jnp.concatenate(
            [value_got[n * count + k, :, :share] for k in range(count)]
            + [value_got[n * count + k, :, share:] for k in range(count)], axis=1
        )
        high, low = pieces(jnp.concatenate([value, jnp.zeros_like(value)]))
        carried = dot(carry_ref[...], jnp.concatenate([high, low, high]))
        gate = gating_ref[:, stretch(n)].astype(F32)
        out_ref[:, stretch(n)] = (gate * (y_buf[:, stretch(n)] + carried)).astype(BF16)

    @pl.loop(0, inner)
    def _(i):
        @pl.when(mine(i))
        def _():
            taps_copy(me, i).wait_send()

    relay_copy(parity).wait_send()
    each_owner(lambda k: part_copy(k, here).wait_send())

    @pl.when(gives)
    def _():
        rates_copy().wait_send()

    @pl.when(owns)
    def _():
        @pl.loop(1, blocks)
        def _(p):
            @pl.when(p != here)
            def _():
                value_copy(p, place).wait_send()


def per_device(signal, gating, decay_rate, residues, skip_gain):
    groups = lax.axis_size("outer")
    inner = lax.axis_size("inner")
    rows, channels = signal.shape
    width, modes = decay_rate.shape
    owners = max(1, min(groups, width // LANES))
    pair = 2 * width // owners
    held = owners * inner // 2
    blocks = groups * inner
    dma = pltpu.SemaphoreType.DMA
    nodes, constants = tables(rows)
    arguments = (
        decay_rate.T, residues.T, signal, gating, skip_gain[None, :],
        *[jnp.asarray(c) for c in constants],
    )

    return pl.pallas_call(
        functools.partial(kernel, groups, inner, owners, modes, nodes),
        out_shape=jax.ShapeDtypeStruct((rows, channels), BF16),
        in_specs=[pl.BlockSpec(memory_space=pltpu.HBM)] * len(arguments),
        out_specs=pl.BlockSpec(memory_space=pltpu.VMEM),
        scratch_shapes=[
            *[pltpu.VMEM(a.shape, a.dtype) for a in arguments],
            pltpu.VMEM((rows, channels), F32),
            pltpu.VMEM((NODES, modes, pair), F32),
            pltpu.VMEM((modes, NODES, pair), F32),
            pltpu.VMEM((NODES, width), F32),
            pltpu.VMEM((2, inner // 2, NODES, width), F32),
            pltpu.VMEM((held, NODES, pair), F32),
            pltpu.VMEM((blocks, NODES, pair), F32),
            pltpu.VMEM((blocks, modes, pair), F32),
            pltpu.VMEM((blocks, NODES, pair), F32),
            pltpu.VMEM((held, NODES, pair), F32),
            pltpu.VMEM((modes, width), F32),
            pltpu.VMEM((2, modes, pair // 2), F32),
            pltpu.VMEM((2, modes, pair // 2), F32),
            pltpu.VMEM((2, modes, pair), F32),
            dma((len(arguments),)),
            dma((inner,)), dma((inner,)), dma(()), dma(()),
            dma((held,)), dma((blocks,)), dma((blocks,)), dma((held,)), dma(()), dma(()),
        ],
        compiler_params=pltpu.CompilerParams(
            collective_id=0, has_side_effects=True, vmem_limit_bytes=24 << 20
        ),
        name="modal_scan",
    )(*[pltpu.with_memory_space_constraint(a, pltpu.HBM) for a in arguments])


def solution(mesh):
    return jax.shard_map(
        per_device,
        mesh=mesh,
        in_specs=(
            P(("outer", "inner"), None),
            P(("outer", "inner"), None),
            P("inner", None),
            P("inner", None),
            P(),
        ),
        out_specs=P(("outer", "inner"), None),
        check_vma=False,
    )
```

```python
import functools

import jax
import jax.numpy as jnp
import numpy as np
from jax import lax
from jax.experimental import pallas as pl
from jax.experimental.pallas import tpu as pltpu
from jax.sharding import PartitionSpec as P

MESH = pl.DeviceIdType.MESH
LANES = 128
F32 = jnp.float32
BF16 = jnp.bfloat16

MOST = 0.05
NODES = 8
NODES_S = (0.00578542, 0.05933078, 0.16499424, 0.31771443,
           0.50753127, 0.70895063, 0.88350275, 0.98635752)
NODES_R = (0.00681489, 0.06128461, 0.17012907, 0.34307065,
           0.48045442, 0.7017412, 0.88152977, 0.98619637)


def wrap(value, size):
    return lax.rem(value + size, size)


def one_minus_exp(z):
    series = jnp.ones_like(z)
    for n in range(12, 1, -1):
        series = 1.0 - series * z * (1.0 / n)
    return jnp.where(z < 0.5, z * series, 1.0 - jnp.exp(-z))


def eliminate(matrix, right):
    matrix, right = matrix.copy(), right.copy()
    size = len(matrix)
    for i in range(size):
        best = i + int(np.argmax(np.abs(matrix[i:, i])))
        matrix[[i, best]], right[[i, best]] = matrix[[best, i]], right[[best, i]]
        for k in range(i + 1, size):
            factor = matrix[k, i] / matrix[i, i]
            matrix[k] -= factor * matrix[i]
            right[k] -= factor * right[i]
    for i in range(size - 1, -1, -1):
        for k in range(i + 1, size):
            right[i] -= matrix[i, k] * right[k]
        right[i] /= matrix[i, i]
    return right


def split(array):
    high = array.astype(jnp.bfloat16)
    low = (array - high.astype(np.float64)).astype(jnp.bfloat16)
    return high, low


def tables(rows):
    assert rows <= 128
    s = np.arange(rows, dtype=np.float64)
    nodes = np.array(NODES_S) * (rows - 1)
    rates = np.array(NODES_R) * MOST
    cards = eliminate(np.exp(-rates[:, None] * nodes), np.exp(-rates[:, None] * s))
    angle = np.pi * (2.0 * s[:, None] + 1.0) / (2.0 * rows) * s[None, :]
    cos, sin = np.cos(angle), np.sin(angle)
    forward = np.concatenate([cos, -sin])
    inverse = np.concatenate([cos.T, -sin.T], axis=1) / rows
    taps = np.zeros((16, rows))
    taps[:NODES] = cards
    taps[NODES, 0] = 1.0
    response = forward @ taps.T
    ends = np.zeros((8, rows))
    ends[:NODES] = cards[:, ::-1]
    carry = np.zeros((rows, 16))
    carry[:, :NODES] = cards.T
    f_high, f_low = split(forward)
    r_high, r_low = split(response)
    i_high, i_low = split(inverse)
    e_high, e_low = split(ends)
    c_high, c_low = split(carry)
    node_rows = np.repeat(nodes[:, None], LANES, axis=1).astype(np.float32)
    return nodes, (
        np.concatenate([f_high, f_low], axis=1),
        np.concatenate([r_high, r_high, r_low], axis=1),
        np.concatenate([i_high, i_low]),
        np.concatenate([e_high, e_low]),
        np.concatenate([c_high, c_high, c_low], axis=1),
        node_rows,
    )


def tree_sum(terms):
    while len(terms) > 1:
        terms = [a + b for a, b in zip(terms[::2], terms[1::2])]
    return terms[0]


def pieces(value):
    high = value.astype(BF16)
    return high, (value - high.astype(F32)).astype(BF16)


def dot(a, b):
    return jnp.dot(a, b, preferred_element_type=F32)


def kernel(
    groups, inner, owners, modes, nodes,
    rate_hbm, residue_hbm, signal_hbm, gating_hbm, skip_hbm,
    forward_hbm, response_hbm, inverse_hbm, ends_hbm, carry_hbm, node_hbm, out_ref,
    rate_ref, residue_ref, signal_ref, gating_ref, skip_ref,
    forward_ref, response_ref, inverse_ref, ends_ref, carry_ref, node_ref,
    y_buf, phi_buf, wphi_buf, taps_own, taps_buf, part_out, part_got, state_buf,
    value_out, value_got, rates_own, rates_got, both_buf,
    load_sem, taps_send, taps_recv, relay_send, relay_recv, part_send, part_recv,
    value_send, value_recv, rates_send, rates_recv,
):
    me = lax.axis_index("inner")
    block = lax.axis_index("outer")
    half = lax.rem(block, 2)
    twin = block + 1 - 2 * half
    rows, channels = signal_ref.shape
    width = rate_ref.shape[1]
    share = width // owners
    blocks = groups * inner
    quarter = inner // 4
    count = owners * quarter
    here = block * inner + me
    first = me < inner // 2
    own_cols = pl.ds(pl.multiple_of(lax.rem(block, owners) * share, LANES), share)

    def owner(g, i):
        return jnp.logical_and(g < owners, jnp.logical_and(i >= quarter, i < 3 * quarter))

    owns = owner(block, me)
    place = (me - quarter) * owners + block

    def others():
        for r in range(inner):
            for g in range(groups):
                if r or g:
                    yield wrap(block + g, groups), wrap(me + r, inner), g * r == 0

    barrier = pltpu.get_barrier_semaphore()
    greeted = jnp.int32(0)
    for g, i, near in others():
        meets = True if near else jnp.logical_or(owns, owner(g, i))
        greeted = greeted + jnp.int32(meets)

        @pl.when(meets)
        def _():
            pl.semaphore_signal(
                barrier, inc=1, device_id={"outer": g, "inner": i}, device_id_type=MESH
            )

    loads = [
        pltpu.make_async_copy(source, target, load_sem.at[n])
        for n, (source, target) in enumerate((
            (rate_hbm, rate_ref), (residue_hbm, residue_ref), (node_hbm, node_ref),
            (ends_hbm, ends_ref), (signal_hbm, signal_ref),
            (forward_hbm, forward_ref), (response_hbm, response_ref),
            (inverse_hbm, inverse_ref), (skip_hbm, skip_ref), (carry_hbm, carry_ref),
            (gating_hbm, gating_ref),
        ))
    ]
    for load in loads:
        load.start()

    def remote(source, target, send, recv, device):
        return pltpu.make_async_remote_copy(
            src_ref=source, dst_ref=target, send_sem=send, recv_sem=recv,
            device_id=device, device_id_type=MESH,
        )

    def taps_copy(source, i):
        return remote(
            taps_own, taps_buf.at[lax.rem(block, owners), source],
            taps_send.at[i], taps_recv.at[source], {"inner": i},
        )

    def relay_copy(q, d):
        return remote(
            taps_buf.at[q], taps_buf.at[q],
            relay_send.at[d], relay_recv.at[q], {"outer": wrap(block + d, groups)},
        )

    def rates_copy():
        i = jnp.where(me < quarter, me + quarter, me - quarter)
        return remote(rates_own, rates_got, rates_send, rates_recv, {"inner": i})

    def part_copy(k, source):
        return remote(
            part_out.at[k], part_got.at[source], part_send.at[k], part_recv.at[source],
            {"outer": k % owners, "inner": quarter + k // owners},
        )

    def value_copy(target, k):
        return remote(
            value_out.at[target], value_got.at[k], value_send.at[target], value_recv.at[k],
            {"outer": target // inner, "inner": target % inner},
        )

    def stretch(n):
        size = channels // 2
        return pl.ds(pl.multiple_of(n * size, LANES), size)

    for n in range(3):
        loads[n].wait()
    rates_own[0] = rate_ref[:, own_cols]
    rates_own[1] = residue_ref[:, own_cols] * jnp.sqrt(one_minus_exp(2.0 * rates_own[0]))
    node_col = jnp.concatenate([node_ref[...]] * (share // LANES), axis=1)
    terms = [
        rates_own[1, m : m + 1, :] * jnp.exp(-(rates_own[0, m : m + 1, :] * node_col))
        for m in range(modes)
    ]
    taps_own[...] = tree_sum(terms)
    shares = block < owners

    @pl.when(shares)
    def _():
        taps_buf[lax.rem(block, owners), me] = taps_own[...]

    gives = jnp.logical_and(block < owners, jnp.logical_not(owns))

    def send_rates():
        @pl.when(gives)
        def _():
            rates_copy().start()

    def send_taps():
        @pl.when(shares)
        def _():
            for r in range(1, inner):
                taps_copy(me, wrap(me + r, inner)).start()

    def sum_parts(n):
        both = dot(ends_ref[...], signal_ref[:, stretch(n)])
        part = both[:NODES] + both[NODES:]
        for k in range(count):
            part_out[n * count + k] = jnp.concatenate([
                part[:, k * share : (k + 1) * share],
                part[:, (count + k) * share : (count + k + 1) * share],
            ], axis=1)

    def each_owner(n, act):
        for k in range(count):
            @pl.when(jnp.logical_or(jnp.logical_not(owns), place != n * count + k))
            def _():
                act(part_copy(n * count + k, here))

    far = jnp.where(first, 1, 0)

    @pl.when(first)
    def _():
        loads[3].wait()
        loads[4].wait()
        sum_parts(far)
        sum_parts(1 - far)
        pl.semaphore_wait(barrier, greeted)
        send_rates()
        each_owner(far, lambda copy: copy.start())
        send_taps()
        each_owner(1 - far, lambda copy: copy.start())

    @pl.when(jnp.logical_not(first))
    def _():
        pl.semaphore_wait(barrier, greeted)
        send_rates()
        send_taps()
        loads[3].wait()
        loads[4].wait()
        sum_parts(far)
        each_owner(far, lambda copy: copy.start())
        sum_parts(1 - far)
        each_owner(1 - far, lambda copy: copy.start())

    @pl.when(owns)
    def _():
        part_got[here] = part_out[place]

        rates_copy().wait_recv()
        for n in range(2):
            got, own = rates_got[n], rates_own[n]
            both_buf[n] = jnp.concatenate(
                [jnp.where(first, got, own), jnp.where(first, own, got)], axis=1
            )
        rate = both_buf[0]
        for j in range(NODES):
            phi_buf[j] = jnp.exp(rate * (-float(nodes[j])))
        node_col = jnp.concatenate([node_ref[...]] * (2 * share // LANES), axis=1)
        for m in range(modes):
            wphi_buf[m] = both_buf[1, m : m + 1, :] * jnp.exp(
                -(both_buf[0, m : m + 1, :] * node_col)
            )

    @pl.when(shares)
    def _():
        for r in range(1, inner):
            taps_copy(wrap(me + r, inner), 0).wait_recv()
        for d in range(1, groups):
            relay_copy(block, d).start()

    @pl.when(owns)
    def _():
        rate = both_buf[0]
        decay_block = jnp.exp(rate * (-float(rows)))
        decay_one = jnp.exp(-rate)

        def advance(p, run):
            @pl.when(p != here)
            def _():
                part_copy(0, p).wait_recv()

            state_buf[p] = decay_one * run
            return decay_block * run + tree_sum(
                [phi_buf[j] * part_got[p, j : j + 1, :] for j in range(NODES)]
            )

        def give(targets):
            for p in targets:
                value_out[p] = tree_sum(
                    [wphi_buf[m] * state_buf[p, m : m + 1, :] for m in range(modes)]
                )

            for p in targets:
                @pl.when(here != p)
                def _():
                    value_copy(p, place).start()

        run = jnp.zeros((modes, 2 * share), F32)
        for g in range(groups):
            if g > 0:
                state_buf[g * inner] = decay_one * run
                give([g * inner])
            run = lax.fori_loop(g * inner, (g + 1) * inner, advance, run, unroll=4)
        for i in range(1, inner):
            give([g * inner + i for g in range(groups)])

        value_got[place] = value_out[here]

    for n in range(5, 11):
        loads[n].wait()

    def local(q):
        for at in range(0, inner, min(8, inner)):
            cols = [
                pl.ds(pl.multiple_of((i * owners + q) * share, LANES), share)
                for i in range(at, at + min(8, inner))
            ]

            def beside(parts):
                return jnp.concatenate(list(parts), axis=1)

            signal = beside(signal_ref[:, c] for c in cols)
            spectrum = dot(forward_ref[...], jnp.concatenate([signal, signal]))
            taps = beside(taps_buf[q, at + n] for n in range(len(cols)))
            filters = jnp.concatenate([
                taps, beside(skip_ref[:, c] for c in cols),
                jnp.zeros((7, taps.shape[1]), F32),
            ])
            high, low = pieces(filters)
            response = dot(response_ref[...], jnp.concatenate([high, low, high]))
            s_re, s_im = spectrum[:rows], spectrum[rows:]
            r_re, r_im = response[:rows], response[rows:]
            product = jnp.concatenate([
                s_re * r_re - s_im * r_im, s_re * r_im + s_im * r_re,
            ])
            high, low = pieces(product)
            two = dot(inverse_ref[...], high)
            one = dot(inverse_ref[:rows], low)
            result = two[:rows] + (two[rows:] + one)
            for n, c in enumerate(cols):
                y_buf[:, c] = result[:, n * share : (n + 1) * share]

    @pl.loop(0, owners)
    def _(step):
        q = step
        if owners == groups:
            q = wrap(jnp.where(step % 2 == 0, block, twin) + step // 2 * 2, groups)

        @pl.when(q != block)
        def _():
            relay_copy(q, 0).wait_recv()

        local(q)

    @pl.when(here == 0)
    def _():
        value_got[...] = jnp.zeros_like(value_got)

    @pl.loop(0, 2)
    def _(step):
        n = jnp.where(first, step, 1 - step)

        @pl.when(here > 0)
        def _():
            @pl.loop(n * count, (n + 1) * count)
            def _(k):
                @pl.when(jnp.logical_or(jnp.logical_not(owns), place != k))
                def _():
                    value_copy(0, k).wait_recv()

        value = jnp.concatenate(
            [value_got[n * count + k, :, :share] for k in range(count)]
            + [value_got[n * count + k, :, share:] for k in range(count)], axis=1
        )
        high, low = pieces(jnp.concatenate([value, jnp.zeros_like(value)]))
        carried = dot(carry_ref[...], jnp.concatenate([high, low, high]))
        gate = gating_ref[:, stretch(n)].astype(F32)
        out_ref[:, stretch(n)] = (gate * (y_buf[:, stretch(n)] + carried)).astype(BF16)

    @pl.when(shares)
    def _():
        for r in range(1, inner):
            taps_copy(me, wrap(me + r, inner)).wait_send()
        for d in range(1, groups):
            relay_copy(block, d).wait_send()

    for n in range(2):
        each_owner(n, lambda copy: copy.wait_send())

    @pl.when(gives)
    def _():
        rates_copy().wait_send()

    @pl.when(owns)
    def _():
        @pl.loop(1, blocks)
        def _(p):
            @pl.when(p != here)
            def _():
                value_copy(p, place).wait_send()


def per_device(signal, gating, decay_rate, residues, skip_gain):
    groups = lax.axis_size("outer")
    inner = lax.axis_size("inner")
    rows, channels = signal.shape
    width, modes = decay_rate.shape
    owners = max(1, min(groups, width // LANES))
    pair = 2 * width // owners
    held = owners * inner // 2
    blocks = groups * inner
    dma = pltpu.SemaphoreType.DMA
    nodes, constants = tables(rows)
    arguments = (
        decay_rate.T, residues.T, signal, gating, skip_gain[None, :],
        *[jnp.asarray(c) for c in constants],
    )

    return pl.pallas_call(
        functools.partial(kernel, groups, inner, owners, modes, nodes),
        out_shape=jax.ShapeDtypeStruct((rows, channels), BF16),
        in_specs=[pl.BlockSpec(memory_space=pltpu.HBM)] * len(arguments),
        out_specs=pl.BlockSpec(memory_space=pltpu.VMEM),
        scratch_shapes=[
            *[pltpu.VMEM(a.shape, a.dtype) for a in arguments],
            pltpu.VMEM((rows, channels), F32),
            pltpu.VMEM((NODES, modes, pair), F32),
            pltpu.VMEM((modes, NODES, pair), F32),
            pltpu.VMEM((NODES, pair // 2), F32),
            pltpu.VMEM((owners, inner, NODES, pair // 2), F32),
            pltpu.VMEM((held, NODES, pair), F32),
            pltpu.VMEM((blocks, NODES, pair), F32),
            pltpu.VMEM((blocks, modes, pair), F32),
            pltpu.VMEM((blocks, NODES, pair), F32),
            pltpu.VMEM((held, NODES, pair), F32),
            pltpu.VMEM((2, modes, pair // 2), F32),
            pltpu.VMEM((2, modes, pair // 2), F32),
            pltpu.VMEM((2, modes, pair), F32),
            dma((len(arguments),)),
            dma((inner,)), dma((inner,)), dma((groups,)), dma((owners,)),
            dma((held,)), dma((blocks,)), dma((blocks,)), dma((held,)), dma(()), dma(()),
        ],
        compiler_params=pltpu.CompilerParams(
            collective_id=0, has_side_effects=True, vmem_limit_bytes=24 << 20
        ),
        name="modal_scan",
    )(*[pltpu.with_memory_space_constraint(a, pltpu.HBM) for a in arguments])


def solution(mesh):
    return jax.shard_map(
        per_device,
        mesh=mesh,
        in_specs=(
            P(("outer", "inner"), None),
            P(("outer", "inner"), None),
            P("inner", None),
            P("inner", None),
            P(),
        ),
        out_specs=P(("outer", "inner"), None),
        check_vma=False,
    )
```

```python
import functools

import jax
import jax.numpy as jnp
import numpy as np
from jax import lax
from jax.experimental import pallas as pl
from jax.experimental.pallas import tpu as pltpu
from jax.sharding import PartitionSpec as P

MESH = pl.DeviceIdType.MESH
LANES = 128
F32 = jnp.float32
BF16 = jnp.bfloat16

MOST = 0.05
NODES = 8
NODES_S = (0.00578542, 0.05933078, 0.16499424, 0.31771443,
           0.50753127, 0.70895063, 0.88350275, 0.98635752)
NODES_R = (0.00681489, 0.06128461, 0.17012907, 0.34307065,
           0.48045442, 0.7017412, 0.88152977, 0.98619637)


def wrap(value, size):
    return lax.rem(value + size, size)


def one_minus_exp(z):
    series = jnp.ones_like(z)
    for n in range(12, 1, -1):
        series = 1.0 - series * z * (1.0 / n)
    return jnp.where(z < 0.5, z * series, 1.0 - jnp.exp(-z))


def eliminate(matrix, right):
    matrix, right = matrix.copy(), right.copy()
    size = len(matrix)
    for i in range(size):
        best = i + int(np.argmax(np.abs(matrix[i:, i])))
        matrix[[i, best]], right[[i, best]] = matrix[[best, i]], right[[best, i]]
        for k in range(i + 1, size):
            factor = matrix[k, i] / matrix[i, i]
            matrix[k] -= factor * matrix[i]
            right[k] -= factor * right[i]
    for i in range(size - 1, -1, -1):
        for k in range(i + 1, size):
            right[i] -= matrix[i, k] * right[k]
        right[i] /= matrix[i, i]
    return right


def split(array):
    high = array.astype(jnp.bfloat16)
    low = (array - high.astype(np.float64)).astype(jnp.bfloat16)
    return high, low


def tables(rows):
    assert rows <= 128
    s = np.arange(rows, dtype=np.float64)
    nodes = np.array(NODES_S) * (rows - 1)
    rates = np.array(NODES_R) * MOST
    cards = eliminate(np.exp(-rates[:, None] * nodes), np.exp(-rates[:, None] * s))
    angle = np.pi * (2.0 * s[:, None] + 1.0) / (2.0 * rows) * s[None, :]
    cos, sin = np.cos(angle), np.sin(angle)
    forward = np.concatenate([cos, -sin])
    inverse = np.concatenate([cos.T, -sin.T], axis=1) / rows
    taps = np.zeros((16, rows))
    taps[:NODES] = cards
    taps[NODES, 0] = 1.0
    response = forward @ taps.T
    ends = np.zeros((8, rows))
    ends[:NODES] = cards[:, ::-1]
    carry = np.zeros((rows, 16))
    carry[:, :NODES] = cards.T
    f_high, f_low = split(forward)
    r_high, r_low = split(response)
    i_high, i_low = split(inverse)
    e_high, e_low = split(ends)
    c_high, c_low = split(carry)
    node_rows = np.repeat(nodes[:, None], LANES, axis=1).astype(np.float32)
    return nodes, (
        np.concatenate([f_high, f_low], axis=1),
        np.concatenate([r_high, r_high, r_low], axis=1),
        np.concatenate([i_high, i_low]),
        np.concatenate([e_high, e_low]),
        np.concatenate([c_high, c_high, c_low], axis=1),
        node_rows,
    )


def tree_sum(terms):
    while len(terms) > 1:
        terms = [a + b for a, b in zip(terms[::2], terms[1::2])]
    return terms[0]


def pieces(value):
    high = value.astype(BF16)
    return high, (value - high.astype(F32)).astype(BF16)


def dot(a, b):
    return jnp.dot(a, b, preferred_element_type=F32)


def kernel(
    groups, inner, owners, modes, nodes,
    rate_hbm, residue_hbm, signal_hbm, gating_hbm, skip_hbm,
    forward_hbm, response_hbm, inverse_hbm, ends_hbm, carry_hbm, node_hbm, out_ref,
    rate_ref, residue_ref, signal_ref, gating_ref, skip_ref,
    forward_ref, response_ref, inverse_ref, ends_ref, carry_ref, node_ref,
    y_buf, phi_buf, wphi_buf, taps_own, taps_buf, part_out, part_got, state_buf,
    value_out, value_got, rates_own, rates_got, both_buf,
    load_sem, taps_send, taps_recv, relay_send, relay_recv, part_send, part_recv,
    value_send, value_recv, rates_send, rates_recv,
):
    me = lax.axis_index("inner")
    block = lax.axis_index("outer")
    half = lax.rem(block, 2)
    twin = block + 1 - 2 * half
    rows, channels = signal_ref.shape
    width = rate_ref.shape[1]
    share = width // owners
    blocks = groups * inner
    quarter = inner // 4
    count = owners * quarter
    here = block * inner + me
    first = me < inner // 2
    own_cols = pl.ds(pl.multiple_of(lax.rem(block, owners) * share, LANES), share)

    def owner(g, i):
        return jnp.logical_and(g < owners, jnp.logical_and(i >= quarter, i < 3 * quarter))

    owns = owner(block, me)
    place = (me - quarter) * owners + block

    barrier = pltpu.get_barrier_semaphore()
    greeted = jnp.int32(0)
    for i in range(inner):
        for g in range(groups):
            meets = jnp.logical_and(here != g * inner + i, jnp.logical_or(
                jnp.logical_or(owns, owner(g, i)), jnp.logical_or(block == g, me == i)
            ))
            greeted = greeted + meets.astype(jnp.int32)

            @pl.when(meets)
            def _():
                pl.semaphore_signal(
                    barrier, inc=1, device_id={"outer": g, "inner": i},
                    device_id_type=MESH,
                )

    loads = [
        pltpu.make_async_copy(source, target, load_sem.at[n])
        for n, (source, target) in enumerate((
            (rate_hbm, rate_ref), (residue_hbm, residue_ref), (node_hbm, node_ref),
            (ends_hbm, ends_ref), (signal_hbm, signal_ref),
            (forward_hbm, forward_ref), (response_hbm, response_ref),
            (inverse_hbm, inverse_ref), (skip_hbm, skip_ref), (carry_hbm, carry_ref),
            (gating_hbm, gating_ref),
        ))
    ]
    for load in loads:
        load.start()

    def remote(source, target, send, recv, device):
        return pltpu.make_async_remote_copy(
            src_ref=source, dst_ref=target, send_sem=send, recv_sem=recv,
            device_id=device, device_id_type=MESH,
        )

    def taps_copy(source, i):
        return remote(
            taps_own, taps_buf.at[lax.rem(block, owners), source],
            taps_send.at[i], taps_recv.at[source], {"inner": i},
        )

    def relay_copy(q, d):
        return remote(
            taps_buf.at[q], taps_buf.at[q],
            relay_send.at[d], relay_recv.at[q], {"outer": wrap(block + d, groups)},
        )

    def rates_copy():
        i = jnp.where(me < quarter, me + quarter, me - quarter)
        return remote(rates_own, rates_got, rates_send, rates_recv, {"inner": i})

    def part_copy(k, source):
        return remote(
            part_out.at[k], part_got.at[source], part_send, part_recv.at[source // inner],
            {"outer": k % owners, "inner": quarter + k // owners},
        )

    def all_parts(g, size):
        here_too = part_got.at[pl.ds(g * inner, size)]
        return remote(here_too, here_too, part_send, part_recv.at[g], {"outer": 0})

    def value_copy(target, k):
        return remote(
            value_out.at[target], value_got.at[k], value_send, value_recv.at[k // count],
            {"outer": target // inner, "inner": target % inner},
        )

    def all_values(n, size):
        here_too = value_got.at[pl.ds(n * count, size)]
        return remote(here_too, here_too, value_send, value_recv.at[n], {"outer": 0})

    def sent(buf, size, semaphore, recv):
        start = buf.at[pl.ds(0, size)]
        remote(start, start, semaphore, recv, {"outer": 0}).wait_send()

    def either(condition, act, yes, no):
        @pl.when(condition)
        def _():
            act(yes)

        @pl.when(jnp.logical_not(condition))
        def _():
            act(no)

    def stretch(n):
        size = channels // 2
        return pl.ds(pl.multiple_of(n * size, LANES), size)

    for n in range(3):
        loads[n].wait()
    rates_own[0] = rate_ref[:, own_cols]
    rates_own[1] = residue_ref[:, own_cols] * jnp.sqrt(one_minus_exp(2.0 * rates_own[0]))
    node_col = jnp.concatenate([node_ref[...]] * (share // LANES), axis=1)
    terms = [
        rates_own[1, m : m + 1, :] * jnp.exp(-(rates_own[0, m : m + 1, :] * node_col))
        for m in range(modes)
    ]
    taps_own[...] = tree_sum(terms)
    shares = block < owners

    @pl.when(shares)
    def _():
        taps_buf[lax.rem(block, owners), me] = taps_own[...]

    gives = jnp.logical_and(block < owners, jnp.logical_not(owns))

    def send_rates():
        @pl.when(gives)
        def _():
            rates_copy().start()

    def send_taps():
        @pl.when(shares)
        def _():
            for r in range(1, inner):
                taps_copy(me, wrap(me + r, inner)).start()

    def sum_parts(n):
        both = dot(ends_ref[...], signal_ref[:, stretch(n)])
        part = both[:NODES] + both[NODES:]
        for k in range(count):
            part_out[n * count + k] = jnp.concatenate([
                part[:, k * share : (k + 1) * share],
                part[:, (count + k) * share : (count + k + 1) * share],
            ], axis=1)

    def each_owner(n, act):
        for k in range(count):
            @pl.when(jnp.logical_or(jnp.logical_not(owns), place != n * count + k))
            def _():
                act(part_copy(n * count + k, here))

    far = jnp.where(first, 1, 0)

    @pl.when(first)
    def _():
        loads[3].wait()
        loads[4].wait()
        sum_parts(far)
        sum_parts(1 - far)
        pl.semaphore_wait(barrier, greeted)

        @pl.when(half == 1)
        def _():
            send_rates()
            send_taps()

        each_owner(far, lambda copy: copy.start())

        @pl.when(half == 0)
        def _():
            send_rates()

        each_owner(1 - far, lambda copy: copy.start())

        @pl.when(half == 0)
        def _():
            send_taps()

    @pl.when(jnp.logical_not(first))
    def _():
        pl.semaphore_wait(barrier, greeted)
        send_rates()
        send_taps()
        loads[3].wait()
        loads[4].wait()
        sum_parts(far)
        each_owner(far, lambda copy: copy.start())
        sum_parts(1 - far)
        each_owner(1 - far, lambda copy: copy.start())

    @pl.when(owns)
    def _():
        part_got[here] = part_out[place]

        rates_copy().wait_recv()
        for n in range(2):
            got, own = rates_got[n], rates_own[n]
            both_buf[n] = jnp.concatenate(
                [jnp.where(first, got, own), jnp.where(first, own, got)], axis=1
            )
        rate = both_buf[0]
        for j in range(NODES):
            phi_buf[j] = jnp.exp(rate * (-float(nodes[j])))
        node_col = jnp.concatenate([node_ref[...]] * (2 * share // LANES), axis=1)
        for m in range(modes):
            wphi_buf[m] = both_buf[1, m : m + 1, :] * jnp.exp(
                -(both_buf[0, m : m + 1, :] * node_col)
            )

    @pl.when(shares)
    def _():
        for r in range(1, inner):
            taps_copy(wrap(me + r, inner), 0).wait_recv()
        for d in range(1, groups):
            relay_copy(block, d).start()

    @pl.when(owns)
    def _():
        rate = both_buf[0]
        decay_block = jnp.exp(rate * (-float(rows)))
        decay_one = jnp.exp(-rate)

        def advance(p, run):
            state_buf[p] = decay_one * run
            return decay_block * run + tree_sum(
                [phi_buf[j] * part_got[p, j : j + 1, :] for j in range(NODES)]
            )

        def give(targets):
            for p in targets:
                value_out[p] = tree_sum(
                    [wphi_buf[m] * state_buf[p, m : m + 1, :] for m in range(modes)]
                )

            for p in targets:
                @pl.when(here != p)
                def _():
                    value_copy(p, place).start()

        run = jnp.zeros((modes, 2 * share), F32)
        for g in range(groups):
            either(
                block == g, lambda size: all_parts(g, size).wait_recv(), inner - 1, inner
            )
            run = lax.fori_loop(g * inner, (g + 1) * inner, advance, run, unroll=4)
            if g + 1 < groups:
                state_buf[(g + 1) * inner] = decay_one * run
                give([(g + 1) * inner])
            for at in range(0, inner, 4):
                give(range(g * inner + max(1, at), g * inner + at + 4))

        value_got[place] = value_out[here]

    for n in range(5, 11):
        loads[n].wait()

    def local(q):
        for at in range(0, inner, min(8, inner)):
            cols = [
                pl.ds(pl.multiple_of((i * owners + q) * share, LANES), share)
                for i in range(at, at + min(8, inner))
            ]

            def beside(parts):
                return jnp.concatenate(list(parts), axis=1)

            signal = beside(signal_ref[:, c] for c in cols)
            spectrum = dot(forward_ref[...], jnp.concatenate([signal, signal]))
            taps = beside(taps_buf[q, at + n] for n in range(len(cols)))
            filters = jnp.concatenate([
                taps, beside(skip_ref[:, c] for c in cols),
                jnp.zeros((7, taps.shape[1]), F32),
            ])
            high, low = pieces(filters)
            response = dot(response_ref[...], jnp.concatenate([high, low, high]))
            s_re, s_im = spectrum[:rows], spectrum[rows:]
            r_re, r_im = response[:rows], response[rows:]
            product = jnp.concatenate([
                s_re * r_re - s_im * r_im, s_re * r_im + s_im * r_re,
            ])
            high, low = pieces(product)
            two = dot(inverse_ref[...], high)
            one = dot(inverse_ref[:rows], low)
            result = two[:rows] + (two[rows:] + one)
            for n, c in enumerate(cols):
                y_buf[:, c] = result[:, n * share : (n + 1) * share]

    @pl.loop(0, owners)
    def _(step):
        q = step
        if owners == groups:
            q = wrap(jnp.where(step % 2 == 0, block, twin) + step // 2 * 2, groups)

        @pl.when(q != block)
        def _():
            relay_copy(q, 0).wait_recv()

        local(q)

    @pl.when(shares)
    def _():
        for r in range(1, inner):
            taps_copy(me, wrap(me + r, inner)).wait_send()
        for d in range(1, groups):
            relay_copy(block, d).wait_send()

    either(
        owns, lambda size: sent(part_out, size, part_send, part_recv.at[0]),
        2 * count - 1, 2 * count,
    )

    @pl.when(gives)
    def _():
        rates_copy().wait_send()

    @pl.when(here == 0)
    def _():
        value_got[...] = jnp.zeros_like(value_got)

    @pl.loop(0, 2)
    def _(step):
        n = jnp.where(first, step, 1 - step)

        @pl.when(here > 0)
        def _():
            either(
                jnp.logical_and(owns, place // count == n),
                lambda size: all_values(n, size).wait_recv(), count - 1, count,
            )

        value = jnp.concatenate(
            [value_got[n * count + k, :, :share] for k in range(count)]
            + [value_got[n * count + k, :, share:] for k in range(count)], axis=1
        )
        high, low = pieces(jnp.concatenate([value, jnp.zeros_like(value)]))
        carried = dot(carry_ref[...], jnp.concatenate([high, low, high]))
        gate = gating_ref[:, stretch(n)].astype(F32)
        out_ref[:, stretch(n)] = (gate * (y_buf[:, stretch(n)] + carried)).astype(BF16)

    @pl.when(owns)
    def _():
        either(
            here > 0, lambda size: sent(value_out, size, value_send, value_recv.at[0]),
            blocks - 2, blocks - 1,
        )


def per_device(signal, gating, decay_rate, residues, skip_gain):
    groups = lax.axis_size("outer")
    inner = lax.axis_size("inner")
    rows, channels = signal.shape
    width, modes = decay_rate.shape
    owners = max(1, min(groups, width // LANES))
    pair = 2 * width // owners
    held = owners * inner // 2
    blocks = groups * inner
    dma = pltpu.SemaphoreType.DMA
    nodes, constants = tables(rows)
    arguments = (
        decay_rate.T, residues.T, signal, gating, skip_gain[None, :],
        *[jnp.asarray(c) for c in constants],
    )

    return pl.pallas_call(
        functools.partial(kernel, groups, inner, owners, modes, nodes),
        out_shape=jax.ShapeDtypeStruct((rows, channels), BF16),
        in_specs=[pl.BlockSpec(memory_space=pltpu.HBM)] * len(arguments),
        out_specs=pl.BlockSpec(memory_space=pltpu.VMEM),
        scratch_shapes=[
            *[pltpu.VMEM(a.shape, a.dtype) for a in arguments],
            pltpu.VMEM((rows, channels), F32),
            pltpu.VMEM((NODES, modes, pair), F32),
            pltpu.VMEM((modes, NODES, pair), F32),
            pltpu.VMEM((NODES, pair // 2), F32),
            pltpu.VMEM((owners, inner, NODES, pair // 2), F32),
            pltpu.VMEM((held, NODES, pair), F32),
            pltpu.VMEM((blocks, NODES, pair), F32),
            pltpu.VMEM((blocks, modes, pair), F32),
            pltpu.VMEM((blocks, NODES, pair), F32),
            pltpu.VMEM((held, NODES, pair), F32),
            pltpu.VMEM((2, modes, pair // 2), F32),
            pltpu.VMEM((2, modes, pair // 2), F32),
            pltpu.VMEM((2, modes, pair), F32),
            dma((len(arguments),)),
            dma((inner,)), dma((inner,)), dma((groups,)), dma((owners,)),
            dma(()), dma((groups,)), dma(()), dma((2,)), dma(()), dma(()),
        ],
        compiler_params=pltpu.CompilerParams(
            collective_id=0, has_side_effects=True, vmem_limit_bytes=24 << 20
        ),
        name="modal_scan",
    )(*[pltpu.with_memory_space_constraint(a, pltpu.HBM) for a in arguments])


def solution(mesh):
    return jax.shard_map(
        per_device,
        mesh=mesh,
        in_specs=(
            P(("outer", "inner"), None),
            P(("outer", "inner"), None),
            P("inner", None),
            P("inner", None),
            P(),
        ),
        out_specs=P(("outer", "inner"), None),
        check_vma=False,
    )
```

```python
import functools

import jax
import jax.numpy as jnp
import numpy as np
from jax import lax
from jax.experimental import pallas as pl
from jax.experimental.pallas import tpu as pltpu
from jax.sharding import PartitionSpec as P

MESH = pl.DeviceIdType.MESH
LANES = 128
F32 = jnp.float32
BF16 = jnp.bfloat16

MOST = 0.05
NODES = 8
NODES_S = (0.00578542, 0.05933078, 0.16499424, 0.31771443,
           0.50753127, 0.70895063, 0.88350275, 0.98635752)
NODES_R = (0.00681489, 0.06128461, 0.17012907, 0.34307065,
           0.48045442, 0.7017412, 0.88152977, 0.98619637)


def wrap(value, size):
    return lax.rem(value + size, size)


def one_minus_exp(z):
    series = jnp.ones_like(z)
    for n in range(12, 1, -1):
        series = 1.0 - series * z * (1.0 / n)
    return jnp.where(z < 0.5, z * series, 1.0 - jnp.exp(-z))


def eliminate(matrix, right):
    matrix, right = matrix.copy(), right.copy()
    size = len(matrix)
    for i in range(size):
        best = i + int(np.argmax(np.abs(matrix[i:, i])))
        matrix[[i, best]], right[[i, best]] = matrix[[best, i]], right[[best, i]]
        for k in range(i + 1, size):
            factor = matrix[k, i] / matrix[i, i]
            matrix[k] -= factor * matrix[i]
            right[k] -= factor * right[i]
    for i in range(size - 1, -1, -1):
        for k in range(i + 1, size):
            right[i] -= matrix[i, k] * right[k]
        right[i] /= matrix[i, i]
    return right


def split(array):
    high = array.astype(jnp.bfloat16)
    low = (array - high.astype(np.float64)).astype(jnp.bfloat16)
    return high, low


def tables(rows):
    assert rows <= 128
    s = np.arange(rows, dtype=np.float64)
    nodes = np.array(NODES_S) * (rows - 1)
    rates = np.array(NODES_R) * MOST
    cards = eliminate(np.exp(-rates[:, None] * nodes), np.exp(-rates[:, None] * s))
    angle = np.pi * (2.0 * s[:, None] + 1.0) / (2.0 * rows) * s[None, :]
    cos, sin = np.cos(angle), np.sin(angle)
    forward = np.concatenate([cos, -sin])
    inverse = np.concatenate([cos.T, -sin.T], axis=1) / rows
    taps = np.zeros((16, rows))
    taps[:NODES] = cards
    taps[NODES, 0] = 1.0
    response = forward @ taps.T
    ends = np.zeros((8, rows))
    ends[:NODES] = cards[:, ::-1]
    carry = np.zeros((rows, 16))
    carry[:, :NODES] = cards.T
    f_high, f_low = split(forward)
    r_high, r_low = split(response)
    i_high, i_low = split(inverse)
    e_high, e_low = split(ends)
    c_high, c_low = split(carry)
    node_rows = np.repeat(nodes[:, None], LANES, axis=1).astype(np.float32)
    return nodes, (
        np.concatenate([f_high, f_low], axis=1),
        np.concatenate([r_high, r_high, r_low], axis=1),
        np.concatenate([i_high, i_low]),
        np.concatenate([e_high, e_low]),
        np.concatenate([c_high, c_high, c_low], axis=1),
        node_rows,
    )


def tree_sum(terms):
    while len(terms) > 1:
        terms = [a + b for a, b in zip(terms[::2], terms[1::2])]
    return terms[0]


def pieces(value):
    high = value.astype(BF16)
    return high, (value - high.astype(F32)).astype(BF16)


def dot(a, b):
    return jnp.dot(a, b, preferred_element_type=F32)


def kernel(
    groups, inner, owners, modes, nodes,
    rate_hbm, residue_hbm, signal_hbm, gating_hbm, skip_hbm,
    forward_hbm, response_hbm, inverse_hbm, ends_hbm, carry_hbm, node_hbm, out_ref,
    rate_ref, residue_ref, signal_ref, gating_ref, skip_ref,
    forward_ref, response_ref, inverse_ref, ends_ref, carry_ref, node_ref,
    y_buf, phi_buf, wphi_buf, taps_own, taps_buf, part_out, part_got, state_buf,
    value_out, value_got, rates_own, rates_got, both_buf,
    load_sem, taps_send, taps_recv, relay_send, relay_recv, part_send, part_recv,
    value_send, value_recv, rates_send, rates_recv,
):
    me = lax.axis_index("inner")
    block = lax.axis_index("outer")
    half = lax.rem(block, 2)
    twin = block + 1 - 2 * half
    rows, channels = signal_ref.shape
    width = rate_ref.shape[1]
    share = width // owners
    blocks = groups * inner
    quarter = inner // 4
    count = owners * quarter
    here = block * inner + me
    first = me < inner // 2
    own_cols = pl.ds(pl.multiple_of(lax.rem(block, owners) * share, LANES), share)

    def owner(g, i):
        return jnp.logical_and(g < owners, jnp.logical_and(i >= quarter, i < 3 * quarter))

    owns = owner(block, me)
    place = (me - quarter) * owners + block

    barrier = pltpu.get_barrier_semaphore()
    greeted = jnp.int32(0)
    for i in range(inner):
        for g in range(groups):
            meets = jnp.logical_and(here != g * inner + i, jnp.logical_or(
                jnp.logical_or(owns, owner(g, i)), jnp.logical_or(block == g, me == i)
            ))
            greeted = greeted + meets.astype(jnp.int32)

            @pl.when(meets)
            def _():
                pl.semaphore_signal(
                    barrier, inc=1, device_id={"outer": g, "inner": i},
                    device_id_type=MESH,
                )

    loads = [
        pltpu.make_async_copy(source, target, load_sem.at[n])
        for n, (source, target) in enumerate((
            (rate_hbm, rate_ref), (residue_hbm, residue_ref), (node_hbm, node_ref),
            (ends_hbm, ends_ref), (signal_hbm, signal_ref),
            (forward_hbm, forward_ref), (response_hbm, response_ref),
            (inverse_hbm, inverse_ref), (skip_hbm, skip_ref), (carry_hbm, carry_ref),
            (gating_hbm, gating_ref),
        ))
    ]
    for load in loads:
        load.start()

    def remote(source, target, send, recv, device):
        return pltpu.make_async_remote_copy(
            src_ref=source, dst_ref=target, send_sem=send, recv_sem=recv,
            device_id=device, device_id_type=MESH,
        )

    def taps_copy(source, i):
        return remote(
            taps_own, taps_buf.at[lax.rem(block, owners), source],
            taps_send, taps_recv, {"inner": i},
        )

    def all_taps():
        start = taps_buf.at[lax.rem(block, owners), pl.ds(0, inner - 1)]
        return remote(start, start, taps_send, taps_recv, {"inner": 0})

    def relay_copy(q, d):
        return remote(
            taps_buf.at[q], taps_buf.at[q],
            relay_send.at[d], relay_recv.at[q], {"outer": wrap(block + d, groups)},
        )

    def rates_copy():
        i = jnp.where(me < quarter, me + quarter, me - quarter)
        return remote(rates_own, rates_got, rates_send, rates_recv, {"inner": i})

    def part_copy(k, source):
        return remote(
            part_out.at[k], part_got.at[source], part_send, part_recv.at[source // inner],
            {"outer": k % owners, "inner": quarter + k // owners},
        )

    def all_parts(g, size):
        here_too = part_got.at[pl.ds(g * inner, size)]
        return remote(here_too, here_too, part_send, part_recv.at[g], {"outer": 0})

    def value_copy(target, k):
        return remote(
            value_out.at[target], value_got.at[k], value_send, value_recv.at[k // count],
            {"outer": target // inner, "inner": target % inner},
        )

    def all_values(n, size):
        here_too = value_got.at[pl.ds(n * count, size)]
        return remote(here_too, here_too, value_send, value_recv.at[n], {"outer": 0})

    def sent(buf, size, semaphore, recv):
        start = buf.at[pl.ds(0, size)]
        remote(start, start, semaphore, recv, {"outer": 0}).wait_send()

    def either(condition, act, yes, no):
        @pl.when(condition)
        def _():
            act(yes)

        @pl.when(jnp.logical_not(condition))
        def _():
            act(no)

    def stretch(n):
        size = channels // 2
        return pl.ds(pl.multiple_of(n * size, LANES), size)

    for n in range(3):
        loads[n].wait()
    rates_own[0] = rate_ref[:, own_cols]
    rates_own[1] = residue_ref[:, own_cols] * jnp.sqrt(one_minus_exp(2.0 * rates_own[0]))
    node_col = jnp.concatenate([node_ref[...]] * (share // LANES), axis=1)
    terms = [
        rates_own[1, m : m + 1, :] * jnp.exp(-(rates_own[0, m : m + 1, :] * node_col))
        for m in range(modes)
    ]
    taps_own[...] = tree_sum(terms)
    shares = block < owners

    @pl.when(shares)
    def _():
        taps_buf[lax.rem(block, owners), me] = taps_own[...]

    gives = jnp.logical_and(block < owners, jnp.logical_not(owns))

    def send_rates():
        @pl.when(gives)
        def _():
            rates_copy().start()

    def send_taps():
        @pl.when(shares)
        def _():
            for r in range(1, inner):
                taps_copy(me, wrap(me + r, inner)).start()

    def sum_parts(n):
        both = dot(ends_ref[...], signal_ref[:, stretch(n)])
        part = both[:NODES] + both[NODES:]
        for k in range(count):
            part_out[n * count + k] = jnp.concatenate([
                part[:, k * share : (k + 1) * share],
                part[:, (count + k) * share : (count + k + 1) * share],
            ], axis=1)

    def send_parts(n):
        @pl.when(owns)
        def _():
            for k in range(count):
                @pl.when(place != n * count + k)
                def _():
                    part_copy(n * count + k, here).start()

        @pl.when(jnp.logical_not(owns))
        def _():
            for k in range(count):
                part_copy(n * count + k, here).start()

    far = jnp.where(first, 1, 0)

    @pl.when(first)
    def _():
        loads[3].wait()
        loads[4].wait()
        sum_parts(far)
        sum_parts(1 - far)
        pl.semaphore_wait(barrier, greeted)

        @pl.when(half == 1)
        def _():
            send_rates()

        send_parts(far)

        @pl.when(half == 0)
        def _():
            send_rates()

        send_parts(1 - far)

        send_taps()

    @pl.when(jnp.logical_not(first))
    def _():
        pl.semaphore_wait(barrier, greeted)
        send_rates()
        send_taps()
        loads[3].wait()
        loads[4].wait()
        sum_parts(far)
        send_parts(far)
        sum_parts(1 - far)
        send_parts(1 - far)

    @pl.when(owns)
    def _():
        part_got[here] = part_out[place]

        rates_copy().wait_recv()
        for n in range(2):
            got, own = rates_got[n], rates_own[n]
            both_buf[n] = jnp.concatenate(
                [jnp.where(first, got, own), jnp.where(first, own, got)], axis=1
            )
        rate = both_buf[0]
        for j in range(NODES):
            phi_buf[j] = jnp.exp(rate * (-float(nodes[j])))
        node_col = jnp.concatenate([node_ref[...]] * (2 * share // LANES), axis=1)
        for m in range(modes):
            wphi_buf[m] = both_buf[1, m : m + 1, :] * jnp.exp(
                -(both_buf[0, m : m + 1, :] * node_col)
            )

    @pl.when(shares)
    def _():
        all_taps().wait_recv()
        for d in range(1, groups):
            relay_copy(block, d).start()

    @pl.when(owns)
    def _():
        rate = both_buf[0]
        decay_block = jnp.exp(rate * (-float(rows)))
        decay_one = jnp.exp(-rate)

        def advance(p, run):
            state_buf[p] = decay_one * run
            return decay_block * run + tree_sum(
                [phi_buf[j] * part_got[p, j : j + 1, :] for j in range(NODES)]
            )

        def give(targets):
            for p in targets:
                value_out[p] = tree_sum(
                    [wphi_buf[m] * state_buf[p, m : m + 1, :] for m in range(modes)]
                )

            for p in targets:
                @pl.when(here != p)
                def _():
                    value_copy(p, place).start()

        run = jnp.zeros((modes, 2 * share), F32)
        for g in range(groups):
            either(
                block == g, lambda size: all_parts(g, size).wait_recv(), inner - 1, inner
            )
            run = lax.fori_loop(g * inner, (g + 1) * inner, advance, run, unroll=4)
            if g + 1 < groups:
                state_buf[(g + 1) * inner] = decay_one * run
                give([(g + 1) * inner])
            for at in range(0, inner, 4):
                give(range(g * inner + max(1, at), g * inner + at + 4))

        value_got[place] = value_out[here]

    for n in range(5, 11):
        loads[n].wait()

    def local(q):
        for at in range(0, inner, min(8, inner)):
            cols = [
                pl.ds(pl.multiple_of((i * owners + q) * share, LANES), share)
                for i in range(at, at + min(8, inner))
            ]

            def beside(parts):
                return jnp.concatenate(list(parts), axis=1)

            signal = beside(signal_ref[:, c] for c in cols)
            spectrum = dot(forward_ref[...], jnp.concatenate([signal, signal]))
            taps = beside(taps_buf[q, at + n] for n in range(len(cols)))
            filters = jnp.concatenate([
                taps, beside(skip_ref[:, c] for c in cols),
                jnp.zeros((7, taps.shape[1]), F32),
            ])
            high, low = pieces(filters)
            response = dot(response_ref[...], jnp.concatenate([high, low, high]))
            s_re, s_im = spectrum[:rows], spectrum[rows:]
            r_re, r_im = response[:rows], response[rows:]
            product = jnp.concatenate([
                s_re * r_re - s_im * r_im, s_re * r_im + s_im * r_re,
            ])
            high, low = pieces(product)
            two = dot(inverse_ref[...], high)
            one = dot(inverse_ref[:rows], low)
            result = two[:rows] + (two[rows:] + one)
            for n, c in enumerate(cols):
                y_buf[:, c] = result[:, n * share : (n + 1) * share]

    @pl.loop(0, owners)
    def _(step):
        q = step
        if owners == groups:
            q = wrap(jnp.where(step % 2 == 0, block, twin) + step // 2 * 2, groups)

        @pl.when(q != block)
        def _():
            relay_copy(q, 0).wait_recv()

        local(q)

    @pl.when(shares)
    def _():
        all_taps().wait_send()
        for d in range(1, groups):
            relay_copy(block, d).wait_send()

    either(
        owns, lambda size: sent(part_out, size, part_send, part_recv.at[0]),
        2 * count - 1, 2 * count,
    )

    @pl.when(gives)
    def _():
        rates_copy().wait_send()

    @pl.when(here == 0)
    def _():
        value_got[...] = jnp.zeros_like(value_got)

    @pl.when(here > 0)
    def _():
        for n in range(2):
            either(
                jnp.logical_and(owns, place // count == n),
                lambda size: all_values(n, size).wait_recv(), count - 1, count,
            )

    for n in range(2):
        cols = slice(n * channels // 2, (n + 1) * channels // 2)
        value = jnp.concatenate(
            [value_got[n * count + k, :, :share] for k in range(count)]
            + [value_got[n * count + k, :, share:] for k in range(count)], axis=1
        )
        high, low = pieces(jnp.concatenate([value, jnp.zeros_like(value)]))
        carried = dot(carry_ref[...], jnp.concatenate([high, low, high]))
        gate = gating_ref[:, cols].astype(F32)
        out_ref[:, cols] = (gate * (y_buf[:, cols] + carried)).astype(BF16)

    @pl.when(owns)
    def _():
        either(
            here > 0, lambda size: sent(value_out, size, value_send, value_recv.at[0]),
            blocks - 2, blocks - 1,
        )


def per_device(signal, gating, decay_rate, residues, skip_gain):
    groups = lax.axis_size("outer")
    inner = lax.axis_size("inner")
    rows, channels = signal.shape
    width, modes = decay_rate.shape
    owners = max(1, min(groups, width // LANES))
    pair = 2 * width // owners
    held = owners * inner // 2
    blocks = groups * inner
    dma = pltpu.SemaphoreType.DMA
    nodes, constants = tables(rows)
    arguments = (
        decay_rate.T, residues.T, signal, gating, skip_gain[None, :],
        *[jnp.asarray(c) for c in constants],
    )

    return pl.pallas_call(
        functools.partial(kernel, groups, inner, owners, modes, nodes),
        out_shape=jax.ShapeDtypeStruct((rows, channels), BF16),
        in_specs=[pl.BlockSpec(memory_space=pltpu.HBM)] * len(arguments),
        out_specs=pl.BlockSpec(memory_space=pltpu.VMEM),
        scratch_shapes=[
            *[pltpu.VMEM(a.shape, a.dtype) for a in arguments],
            pltpu.VMEM((rows, channels), F32),
            pltpu.VMEM((NODES, modes, pair), F32),
            pltpu.VMEM((modes, NODES, pair), F32),
            pltpu.VMEM((NODES, pair // 2), F32),
            pltpu.VMEM((owners, inner, NODES, pair // 2), F32),
            pltpu.VMEM((held, NODES, pair), F32),
            pltpu.VMEM((blocks, NODES, pair), F32),
            pltpu.VMEM((blocks, modes, pair), F32),
            pltpu.VMEM((blocks, NODES, pair), F32),
            pltpu.VMEM((held, NODES, pair), F32),
            pltpu.VMEM((2, modes, pair // 2), F32),
            pltpu.VMEM((2, modes, pair // 2), F32),
            pltpu.VMEM((2, modes, pair), F32),
            dma((len(arguments),)),
            dma(()), dma(()), dma((groups,)), dma((owners,)),
            dma(()), dma((groups,)), dma(()), dma((2,)), dma(()), dma(()),
        ],
        compiler_params=pltpu.CompilerParams(
            collective_id=0, has_side_effects=True, vmem_limit_bytes=24 << 20
        ),
        name="modal_scan",
    )(*[pltpu.with_memory_space_constraint(a, pltpu.HBM) for a in arguments])


def solution(mesh):
    return jax.shard_map(
        per_device,
        mesh=mesh,
        in_specs=(
            P(("outer", "inner"), None),
            P(("outer", "inner"), None),
            P("inner", None),
            P("inner", None),
            P(),
        ),
        out_specs=P(("outer", "inner"), None),
        check_vma=False,
    )
```

```python
import functools

import jax
import jax.numpy as jnp
import numpy as np
from jax import lax
from jax.experimental import pallas as pl
from jax.experimental.pallas import tpu as pltpu
from jax.sharding import PartitionSpec as P

MESH = pl.DeviceIdType.MESH
LANES = 128
F32 = jnp.float32
BF16 = jnp.bfloat16

MOST = 0.05
NODES = 8
NODES_S = (0.00578542, 0.05933078, 0.16499424, 0.31771443,
           0.50753127, 0.70895063, 0.88350275, 0.98635752)
NODES_R = (0.00681489, 0.06128461, 0.17012907, 0.34307065,
           0.48045442, 0.7017412, 0.88152977, 0.98619637)


def wrap(value, size):
    return lax.rem(value + size, size)


def one_minus_exp(z):
    series = jnp.ones_like(z)
    for n in range(12, 1, -1):
        series = 1.0 - series * z * (1.0 / n)
    return jnp.where(z < 0.5, z * series, 1.0 - jnp.exp(-z))


def eliminate(matrix, right):
    matrix, right = matrix.copy(), right.copy()
    size = len(matrix)
    for i in range(size):
        best = i + int(np.argmax(np.abs(matrix[i:, i])))
        matrix[[i, best]], right[[i, best]] = matrix[[best, i]], right[[best, i]]
        for k in range(i + 1, size):
            factor = matrix[k, i] / matrix[i, i]
            matrix[k] -= factor * matrix[i]
            right[k] -= factor * right[i]
    for i in range(size - 1, -1, -1):
        for k in range(i + 1, size):
            right[i] -= matrix[i, k] * right[k]
        right[i] /= matrix[i, i]
    return right


def split(array):
    high = array.astype(jnp.bfloat16)
    low = (array - high.astype(np.float64)).astype(jnp.bfloat16)
    return high, low


def tables(rows):
    assert rows <= 128
    s = np.arange(rows, dtype=np.float64)
    nodes = np.array(NODES_S) * (rows - 1)
    rates = np.array(NODES_R) * MOST
    cards = eliminate(np.exp(-rates[:, None] * nodes), np.exp(-rates[:, None] * s))
    angle = np.pi * (2.0 * s[:, None] + 1.0) / (2.0 * rows) * s[None, :]
    cos, sin = np.cos(angle), np.sin(angle)
    forward = np.concatenate([cos, -sin])
    inverse = np.concatenate([cos.T, -sin.T], axis=1) / rows
    taps = np.zeros((16, rows))
    taps[:NODES] = cards
    taps[NODES, 0] = 1.0
    response = forward @ taps.T
    ends = np.zeros((8, rows))
    ends[:NODES] = cards[:, ::-1]
    carry = np.zeros((rows, 16))
    carry[:, :NODES] = cards.T
    f_high, f_low = split(forward)
    r_high, r_low = split(response)
    i_high, i_low = split(inverse)
    e_high, e_low = split(ends)
    c_high, c_low = split(carry)
    node_rows = np.repeat(nodes[:, None], LANES, axis=1).astype(np.float32)
    return nodes, (
        np.concatenate([f_high, f_low], axis=1),
        np.concatenate([r_high, r_high, r_low], axis=1),
        np.concatenate([i_high, i_low]),
        np.concatenate([e_high, e_low]),
        np.concatenate([c_high, c_high, c_low], axis=1),
        node_rows,
    )


def tree_sum(terms):
    while len(terms) > 1:
        terms = [a + b for a, b in zip(terms[::2], terms[1::2])]
    return terms[0]


def pieces(value):
    high = value.astype(BF16)
    return high, (value - high.astype(F32)).astype(BF16)


def dot(a, b):
    return jnp.dot(a, b, preferred_element_type=F32)


def kernel(
    groups, inner, owners, modes, nodes,
    rate_hbm, residue_hbm, signal_hbm, gating_hbm, skip_hbm,
    forward_hbm, response_hbm, inverse_hbm, ends_hbm, carry_hbm, node_hbm, out_ref,
    rate_ref, residue_ref, signal_ref, gating_ref, skip_ref,
    forward_ref, response_ref, inverse_ref, ends_ref, carry_ref, node_ref,
    y_buf, phi_buf, wphi_buf, taps_own, taps_buf, part_out, part_got, state_buf,
    value_out, value_got, rates_own, rates_got, both_buf,
    load_sem, taps_send, taps_recv, relay_send, relay_recv, part_send, part_recv,
    value_send, value_recv, rates_send, rates_recv,
):
    me = lax.axis_index("inner")
    block = lax.axis_index("outer")
    half = lax.rem(block, 2)
    twin = block + 1 - 2 * half
    rows, channels = signal_ref.shape
    width = rate_ref.shape[1]
    share = width // owners
    blocks = groups * inner
    quarter = inner // 4
    count = owners * quarter
    here = block * inner + me
    first = me < inner // 2
    own_cols = pl.ds(pl.multiple_of(lax.rem(block, owners) * share, LANES), share)

    def owner(g, i):
        return jnp.logical_and(g < owners, jnp.logical_and(i >= quarter, i < 3 * quarter))

    owns = owner(block, me)
    place = (me - quarter) * owners + block

    barrier = pltpu.get_barrier_semaphore()
    greeted = jnp.int32(0)
    for i in range(inner):
        for g in range(groups):
            meets = jnp.logical_and(here != g * inner + i, jnp.logical_or(
                jnp.logical_or(owns, owner(g, i)), jnp.logical_or(block == g, me == i)
            ))
            greeted = greeted + meets.astype(jnp.int32)

            @pl.when(meets)
            def _():
                pl.semaphore_signal(
                    barrier, inc=1, device_id={"outer": g, "inner": i},
                    device_id_type=MESH,
                )

    loads = [
        pltpu.make_async_copy(source, target, load_sem.at[n])
        for n, (source, target) in enumerate((
            (rate_hbm, rate_ref), (residue_hbm, residue_ref), (node_hbm, node_ref),
            (ends_hbm, ends_ref), (signal_hbm, signal_ref),
            (forward_hbm, forward_ref), (response_hbm, response_ref),
            (inverse_hbm, inverse_ref), (skip_hbm, skip_ref), (carry_hbm, carry_ref),
            (gating_hbm, gating_ref),
        ))
    ]
    for load in loads:
        load.start()

    def remote(source, target, send, recv, device):
        return pltpu.make_async_remote_copy(
            src_ref=source, dst_ref=target, send_sem=send, recv_sem=recv,
            device_id=device, device_id_type=MESH,
        )

    def taps_copy(source, i):
        return remote(
            taps_own, taps_buf.at[lax.rem(block, owners), source],
            taps_send, taps_recv, {"inner": i},
        )

    def all_taps():
        start = taps_buf.at[lax.rem(block, owners), pl.ds(0, inner - 1)]
        return remote(start, start, taps_send, taps_recv, {"inner": 0})

    def relay_copy(q, d):
        return remote(
            taps_buf.at[q], taps_buf.at[q],
            relay_send.at[d], relay_recv.at[q], {"outer": wrap(block + d, groups)},
        )

    def rates_copy():
        i = jnp.where(me < quarter, me + quarter, me - quarter)
        return remote(rates_own, rates_got, rates_send, rates_recv, {"inner": i})

    def part_copy(k, source):
        return remote(
            part_out.at[k], part_got.at[source], part_send, part_recv.at[source // inner],
            {"outer": k % owners, "inner": quarter + k // owners},
        )

    def all_parts(g, size):
        here_too = part_got.at[pl.ds(g * inner, size)]
        return remote(here_too, here_too, part_send, part_recv.at[g], {"outer": 0})

    def value_copy(target, k):
        return remote(
            value_out.at[target], value_got.at[k], value_send, value_recv.at[k // count],
            {"outer": target // inner, "inner": target % inner},
        )

    def all_values(n, size):
        here_too = value_got.at[pl.ds(n * count, size)]
        return remote(here_too, here_too, value_send, value_recv.at[n], {"outer": 0})

    def sent(buf, size, semaphore, recv):
        start = buf.at[pl.ds(0, size)]
        remote(start, start, semaphore, recv, {"outer": 0}).wait_send()

    def either(condition, act, yes, no):
        @pl.when(condition)
        def _():
            act(yes)

        @pl.when(jnp.logical_not(condition))
        def _():
            act(no)

    def stretch(n):
        size = channels // 2
        return pl.ds(pl.multiple_of(n * size, LANES), size)

    for n in range(3):
        loads[n].wait()
    rates_own[0] = rate_ref[:, own_cols]
    rates_own[1] = residue_ref[:, own_cols] * jnp.sqrt(one_minus_exp(2.0 * rates_own[0]))
    node_col = jnp.concatenate([node_ref[...]] * (share // LANES), axis=1)
    terms = [
        rates_own[1, m : m + 1, :] * jnp.exp(-(rates_own[0, m : m + 1, :] * node_col))
        for m in range(modes)
    ]
    taps_own[...] = tree_sum(terms)
    shares = block < owners

    @pl.when(shares)
    def _():
        taps_buf[lax.rem(block, owners), me] = taps_own[...]

    gives = jnp.logical_and(block < owners, jnp.logical_not(owns))

    def send_rates():
        @pl.when(gives)
        def _():
            rates_copy().start()

    def send_taps():
        @pl.when(shares)
        def _():
            for r in range(1, inner):
                taps_copy(me, wrap(me + r, inner)).start()

    def sum_parts(n):
        both = dot(ends_ref[...], signal_ref[:, stretch(n)])
        part = both[:NODES] + both[NODES:]
        for k in range(count):
            part_out[n * count + k] = jnp.concatenate([
                part[:, k * share : (k + 1) * share],
                part[:, (count + k) * share : (count + k + 1) * share],
            ], axis=1)

    def send_parts(n):
        @pl.when(owns)
        def _():
            for k in range(count):
                @pl.when(place != n * count + k)
                def _():
                    part_copy(n * count + k, here).start()

        @pl.when(jnp.logical_not(owns))
        def _():
            for k in range(count):
                part_copy(n * count + k, here).start()

    far = jnp.where(first, 1, 0)

    @pl.when(first)
    def _():
        loads[3].wait()
        loads[4].wait()
        sum_parts(far)
        sum_parts(1 - far)
        pl.semaphore_wait(barrier, greeted)

        send_parts(far)
        send_rates()
        send_taps()
        send_parts(1 - far)

    @pl.when(jnp.logical_not(first))
    def _():
        pl.semaphore_wait(barrier, greeted)
        send_rates()
        send_taps()
        loads[3].wait()
        loads[4].wait()
        sum_parts(far)
        send_parts(far)
        sum_parts(1 - far)
        send_parts(1 - far)

    @pl.when(owns)
    def _():
        part_got[here] = part_out[place]

        rates_copy().wait_recv()
        for n in range(2):
            got, own = rates_got[n], rates_own[n]
            both_buf[n] = jnp.concatenate(
                [jnp.where(first, got, own), jnp.where(first, own, got)], axis=1
            )
        rate = both_buf[0]
        for j in range(NODES):
            phi_buf[j] = jnp.exp(rate * (-float(nodes[j])))
        node_col = jnp.concatenate([node_ref[...]] * (2 * share // LANES), axis=1)
        for m in range(modes):
            wphi_buf[m] = both_buf[1, m : m + 1, :] * jnp.exp(
                -(both_buf[0, m : m + 1, :] * node_col)
            )

    @pl.when(shares)
    def _():
        all_taps().wait_recv()
        for d in range(1, groups):
            relay_copy(block, d).start()

    @pl.when(owns)
    def _():
        rate = both_buf[0]
        decay_block = jnp.exp(rate * (-float(rows)))
        decay_one = jnp.exp(-rate)

        def advance(p, run):
            state_buf[p] = decay_one * run
            return decay_block * run + tree_sum(
                [phi_buf[j] * part_got[p, j : j + 1, :] for j in range(NODES)]
            )

        def give(targets):
            for p in targets:
                value_out[p] = tree_sum(
                    [wphi_buf[m] * state_buf[p, m : m + 1, :] for m in range(modes)]
                )

            for p in targets:
                @pl.when(here != p)
                def _():
                    value_copy(p, place).start()

        run = jnp.zeros((modes, 2 * share), F32)
        for g in range(groups):
            either(
                block == g, lambda size: all_parts(g, size).wait_recv(), inner - 1, inner
            )
            run = lax.fori_loop(g * inner, (g + 1) * inner, advance, run, unroll=4)
            if g + 1 < groups:
                state_buf[(g + 1) * inner] = decay_one * run
                give([(g + 1) * inner])
            for at in range(0, inner, 4):
                give(range(g * inner + max(1, at), g * inner + at + 4))

        value_got[place] = value_out[here]

    for n in range(5, 11):
        loads[n].wait()

    def local(q):
        for at in range(0, inner, min(8, inner)):
            cols = [
                pl.ds(pl.multiple_of((i * owners + q) * share, LANES), share)
                for i in range(at, at + min(8, inner))
            ]

            def beside(parts):
                return jnp.concatenate(list(parts), axis=1)

            signal = beside(signal_ref[:, c] for c in cols)
            spectrum = dot(forward_ref[...], jnp.concatenate([signal, signal]))
            taps = beside(taps_buf[q, at + n] for n in range(len(cols)))
            filters = jnp.concatenate([
                taps, beside(skip_ref[:, c] for c in cols),
                jnp.zeros((7, taps.shape[1]), F32),
            ])
            high, low = pieces(filters)
            response = dot(response_ref[...], jnp.concatenate([high, low, high]))
            s_re, s_im = spectrum[:rows], spectrum[rows:]
            r_re, r_im = response[:rows], response[rows:]
            product = jnp.concatenate([
                s_re * r_re - s_im * r_im, s_re * r_im + s_im * r_re,
            ])
            high, low = pieces(product)
            two = dot(inverse_ref[...], high)
            one = dot(inverse_ref[:rows], low)
            result = two[:rows] + (two[rows:] + one)
            for n, c in enumerate(cols):
                y_buf[:, c] = result[:, n * share : (n + 1) * share]

    @pl.loop(0, owners)
    def _(step):
        q = step
        if owners == groups:
            q = wrap(jnp.where(step % 2 == 0, block, twin) + step // 2 * 2, groups)

        @pl.when(q != block)
        def _():
            relay_copy(q, 0).wait_recv()

        local(q)

    @pl.when(shares)
    def _():
        all_taps().wait_send()
        for d in range(1, groups):
            relay_copy(block, d).wait_send()

    either(
        owns, lambda size: sent(part_out, size, part_send, part_recv.at[0]),
        2 * count - 1, 2 * count,
    )

    @pl.when(gives)
    def _():
        rates_copy().wait_send()

    @pl.when(here == 0)
    def _():
        value_got[...] = jnp.zeros_like(value_got)

    @pl.when(here > 0)
    def _():
        for n in range(2):
            either(
                jnp.logical_and(owns, place // count == n),
                lambda size: all_values(n, size).wait_recv(), count - 1, count,
            )

    for n in range(2):
        cols = slice(n * channels // 2, (n + 1) * channels // 2)
        value = jnp.concatenate(
            [value_got[n * count + k, :, :share] for k in range(count)]
            + [value_got[n * count + k, :, share:] for k in range(count)], axis=1
        )
        high, low = pieces(jnp.concatenate([value, jnp.zeros_like(value)]))
        carried = dot(carry_ref[...], jnp.concatenate([high, low, high]))
        gate = gating_ref[:, cols].astype(F32)
        out_ref[:, cols] = (gate * (y_buf[:, cols] + carried)).astype(BF16)

    @pl.when(owns)
    def _():
        either(
            here > 0, lambda size: sent(value_out, size, value_send, value_recv.at[0]),
            blocks - 2, blocks - 1,
        )


def per_device(signal, gating, decay_rate, residues, skip_gain):
    groups = lax.axis_size("outer")
    inner = lax.axis_size("inner")
    rows, channels = signal.shape
    width, modes = decay_rate.shape
    owners = max(1, min(groups, width // LANES))
    pair = 2 * width // owners
    held = owners * inner // 2
    blocks = groups * inner
    dma = pltpu.SemaphoreType.DMA
    nodes, constants = tables(rows)
    arguments = (
        decay_rate.T, residues.T, signal, gating, skip_gain[None, :],
        *[jnp.asarray(c) for c in constants],
    )

    return pl.pallas_call(
        functools.partial(kernel, groups, inner, owners, modes, nodes),
        out_shape=jax.ShapeDtypeStruct((rows, channels), BF16),
        in_specs=[pl.BlockSpec(memory_space=pltpu.HBM)] * len(arguments),
        out_specs=pl.BlockSpec(memory_space=pltpu.VMEM),
        scratch_shapes=[
            *[pltpu.VMEM(a.shape, a.dtype) for a in arguments],
            pltpu.VMEM((rows, channels), F32),
            pltpu.VMEM((NODES, modes, pair), F32),
            pltpu.VMEM((modes, NODES, pair), F32),
            pltpu.VMEM((NODES, pair // 2), F32),
            pltpu.VMEM((owners, inner, NODES, pair // 2), F32),
            pltpu.VMEM((held, NODES, pair), F32),
            pltpu.VMEM((blocks, NODES, pair), F32),
            pltpu.VMEM((blocks, modes, pair), F32),
            pltpu.VMEM((blocks, NODES, pair), F32),
            pltpu.VMEM((held, NODES, pair), F32),
            pltpu.VMEM((2, modes, pair // 2), F32),
            pltpu.VMEM((2, modes, pair // 2), F32),
            pltpu.VMEM((2, modes, pair), F32),
            dma((len(arguments),)),
            dma(()), dma(()), dma((groups,)), dma((owners,)),
            dma(()), dma((groups,)), dma(()), dma((2,)), dma(()), dma(()),
        ],
        compiler_params=pltpu.CompilerParams(
            collective_id=0, has_side_effects=True, vmem_limit_bytes=24 << 20
        ),
        name="modal_scan",
    )(*[pltpu.with_memory_space_constraint(a, pltpu.HBM) for a in arguments])


def solution(mesh):
    return jax.shard_map(
        per_device,
        mesh=mesh,
        in_specs=(
            P(("outer", "inner"), None),
            P(("outer", "inner"), None),
            P("inner", None),
            P("inner", None),
            P(),
        ),
        out_specs=P(("outer", "inner"), None),
        check_vma=False,
    )
```

```python
import functools

import jax
import jax.numpy as jnp
import numpy as np
from jax import lax
from jax.experimental import pallas as pl
from jax.experimental.pallas import tpu as pltpu
from jax.sharding import PartitionSpec as P

MESH = pl.DeviceIdType.MESH
LANES = 128
F32 = jnp.float32
BF16 = jnp.bfloat16

MOST = 0.05
NODES = 8
NODES_S = (0.00578542, 0.05933078, 0.16499424, 0.31771443,
           0.50753127, 0.70895063, 0.88350275, 0.98635752)
NODES_R = (0.00681489, 0.06128461, 0.17012907, 0.34307065,
           0.48045442, 0.7017412, 0.88152977, 0.98619637)


def wrap(value, size):
    return lax.rem(value + size, size)


def one_minus_exp(z):
    series = jnp.ones_like(z)
    for n in range(12, 1, -1):
        series = 1.0 - series * z * (1.0 / n)
    return jnp.where(z < 0.5, z * series, 1.0 - jnp.exp(-z))


def eliminate(matrix, right):
    matrix, right = matrix.copy(), right.copy()
    size = len(matrix)
    for i in range(size):
        best = i + int(np.argmax(np.abs(matrix[i:, i])))
        matrix[[i, best]], right[[i, best]] = matrix[[best, i]], right[[best, i]]
        for k in range(i + 1, size):
            factor = matrix[k, i] / matrix[i, i]
            matrix[k] -= factor * matrix[i]
            right[k] -= factor * right[i]
    for i in range(size - 1, -1, -1):
        for k in range(i + 1, size):
            right[i] -= matrix[i, k] * right[k]
        right[i] /= matrix[i, i]
    return right


def split(array):
    high = array.astype(jnp.bfloat16)
    low = (array - high.astype(np.float64)).astype(jnp.bfloat16)
    return high, low


def tables(rows):
    assert rows <= 128
    s = np.arange(rows, dtype=np.float64)
    nodes = np.array(NODES_S) * (rows - 1)
    rates = np.array(NODES_R) * MOST
    cards = eliminate(np.exp(-rates[:, None] * nodes), np.exp(-rates[:, None] * s))
    angle = np.pi * (2.0 * s[:, None] + 1.0) / (2.0 * rows) * s[None, :]
    cos, sin = np.cos(angle), np.sin(angle)
    forward = np.concatenate([cos, -sin])
    inverse = np.concatenate([cos.T, -sin.T], axis=1) / rows
    taps = np.zeros((16, rows))
    taps[:NODES] = cards
    taps[NODES, 0] = 1.0
    response = forward @ taps.T
    ends = np.zeros((8, rows))
    ends[:NODES] = cards[:, ::-1]
    carry = np.zeros((rows, 16))
    carry[:, :NODES] = cards.T
    f_high, f_low = split(forward)
    r_high, r_low = split(response)
    i_high, i_low = split(inverse)
    e_high, e_low = split(ends)
    c_high, c_low = split(carry)
    node_rows = np.repeat(nodes[:, None], LANES, axis=1).astype(np.float32)
    return nodes, (
        np.concatenate([f_high, f_low], axis=1),
        np.concatenate([r_high, r_high, r_low], axis=1),
        np.concatenate([i_high, i_low]),
        np.concatenate([e_high, e_low]),
        np.concatenate([c_high, c_high, c_low], axis=1),
        node_rows,
    )


def tree_sum(terms):
    while len(terms) > 1:
        terms = [a + b for a, b in zip(terms[::2], terms[1::2])]
    return terms[0]


def pieces(value):
    high = value.astype(BF16)
    return high, (value - high.astype(F32)).astype(BF16)


def dot(a, b):
    return jnp.dot(a, b, preferred_element_type=F32)


def kernel(
    groups, inner, owners, modes, nodes,
    rate_hbm, residue_hbm, signal_hbm, gating_hbm, skip_hbm,
    forward_hbm, response_hbm, inverse_hbm, ends_hbm, carry_hbm, node_hbm, out_ref,
    rate_ref, residue_ref, signal_ref, gating_ref, skip_ref,
    forward_ref, response_ref, inverse_ref, ends_ref, carry_ref, node_ref,
    y_buf, phi_buf, wphi_buf, taps_own, taps_buf, part_out, part_got, state_buf,
    value_out, value_got, rates_own, rates_got, both_buf,
    load_sem, taps_send, taps_recv, relay_send, relay_recv, part_send, part_recv,
    value_send, value_recv, rates_send, rates_recv,
):
    me = lax.axis_index("inner")
    block = lax.axis_index("outer")
    half = lax.rem(block, 2)
    twin = block + 1 - 2 * half
    rows, channels = signal_ref.shape
    width = rate_ref.shape[1]
    share = width // owners
    blocks = groups * inner
    quarter = inner // 4
    count = owners * quarter
    here = block * inner + me
    first = me < inner // 2
    own_cols = pl.ds(pl.multiple_of(lax.rem(block, owners) * share, LANES), share)

    def owner(g, i):
        return jnp.logical_and(g < owners, jnp.logical_and(i >= quarter, i < 3 * quarter))

    owns = owner(block, me)
    place = (me - quarter) * owners + block

    def others():
        for r in range(inner):
            for g in range(groups):
                if r or g:
                    yield wrap(block + g, groups), wrap(me + r, inner), g * r == 0

    barrier = pltpu.get_barrier_semaphore()
    greeted = jnp.int32(0)
    for g, i, near in others():
        meets = True if near else jnp.logical_or(owns, owner(g, i))
        greeted = greeted + jnp.int32(meets)

        @pl.when(meets)
        def _():
            pl.semaphore_signal(
                barrier, inc=1, device_id={"outer": g, "inner": i}, device_id_type=MESH
            )

    loads = [
        pltpu.make_async_copy(source, target, load_sem.at[n])
        for n, (source, target) in enumerate((
            (rate_hbm, rate_ref), (residue_hbm, residue_ref), (node_hbm, node_ref),
            (ends_hbm, ends_ref), (signal_hbm, signal_ref),
            (forward_hbm, forward_ref), (response_hbm, response_ref),
            (inverse_hbm, inverse_ref), (skip_hbm, skip_ref), (carry_hbm, carry_ref),
            (gating_hbm, gating_ref),
        ))
    ]
    for load in loads:
        load.start()

    def remote(source, target, send, recv, device):
        return pltpu.make_async_remote_copy(
            src_ref=source, dst_ref=target, send_sem=send, recv_sem=recv,
            device_id=device, device_id_type=MESH,
        )

    def taps_copy(source, i):
        return remote(
            taps_own, taps_buf.at[lax.rem(block, owners), source],
            taps_send, taps_recv, {"inner": i},
        )

    def all_taps():
        start = taps_buf.at[lax.rem(block, owners), pl.ds(0, inner - 1)]
        return remote(start, start, taps_send, taps_recv, {"inner": 0})

    def relay_copy(q, d):
        return remote(
            taps_buf.at[q], taps_buf.at[q],
            relay_send.at[d], relay_recv.at[q], {"outer": wrap(block + d, groups)},
        )

    def rates_copy():
        i = jnp.where(me < quarter, me + quarter, me - quarter)
        return remote(rates_own, rates_got, rates_send, rates_recv, {"inner": i})

    def part_copy(k, source):
        return remote(
            part_out.at[k], part_got.at[source], part_send, part_recv.at[source // inner],
            {"outer": k % owners, "inner": quarter + k // owners},
        )

    def all_parts(g, size):
        here_too = part_got.at[pl.ds(g * inner, size)]
        return remote(here_too, here_too, part_send, part_recv.at[g], {"outer": 0})

    def value_copy(target, k):
        return remote(
            value_out.at[target], value_got.at[k], value_send, value_recv.at[k // count],
            {"outer": target // inner, "inner": target % inner},
        )

    def all_values(n, size):
        here_too = value_got.at[pl.ds(n * count, size)]
        return remote(here_too, here_too, value_send, value_recv.at[n], {"outer": 0})

    def sent(buf, size, semaphore, recv):
        start = buf.at[pl.ds(0, size)]
        remote(start, start, semaphore, recv, {"outer": 0}).wait_send()

    def either(condition, act, yes, no):
        @pl.when(condition)
        def _():
            act(yes)

        @pl.when(jnp.logical_not(condition))
        def _():
            act(no)

    def stretch(n):
        size = channels // 2
        return pl.ds(pl.multiple_of(n * size, LANES), size)

    for n in range(3):
        loads[n].wait()
    rates_own[0] = rate_ref[:, own_cols]
    rates_own[1] = residue_ref[:, own_cols] * jnp.sqrt(one_minus_exp(2.0 * rates_own[0]))
    node_col = jnp.concatenate([node_ref[...]] * (share // LANES), axis=1)
    terms = [
        rates_own[1, m : m + 1, :] * jnp.exp(-(rates_own[0, m : m + 1, :] * node_col))
        for m in range(modes)
    ]
    taps_own[...] = tree_sum(terms)
    shares = block < owners

    @pl.when(shares)
    def _():
        taps_buf[lax.rem(block, owners), me] = taps_own[...]

    gives = jnp.logical_and(block < owners, jnp.logical_not(owns))

    def send_rates():
        @pl.when(gives)
        def _():
            rates_copy().start()

    def send_taps():
        @pl.when(shares)
        def _():
            for r in range(1, inner):
                taps_copy(me, wrap(me + r, inner)).start()

    def sum_parts(n):
        both = dot(ends_ref[...], signal_ref[:, stretch(n)])
        part = both[:NODES] + both[NODES:]
        for k in range(count):
            part_out[n * count + k] = jnp.concatenate([
                part[:, k * share : (k + 1) * share],
                part[:, (count + k) * share : (count + k + 1) * share],
            ], axis=1)

    def send_parts(n):
        @pl.when(owns)
        def _():
            for k in range(count):
                @pl.when(place != n * count + k)
                def _():
                    part_copy(n * count + k, here).start()

        @pl.when(jnp.logical_not(owns))
        def _():
            for k in range(count):
                part_copy(n * count + k, here).start()

    far = jnp.where(first, 1, 0)

    @pl.when(first)
    def _():
        loads[3].wait()
        loads[4].wait()
        sum_parts(far)
        sum_parts(1 - far)
        pl.semaphore_wait(barrier, greeted)

        send_parts(far)
        send_rates()
        send_taps()
        send_parts(1 - far)

    @pl.when(jnp.logical_not(first))
    def _():
        pl.semaphore_wait(barrier, greeted)
        send_rates()
        send_taps()
        loads[3].wait()
        loads[4].wait()
        sum_parts(far)
        send_parts(far)
        sum_parts(1 - far)
        send_parts(1 - far)

    @pl.when(owns)
    def _():
        part_got[here] = part_out[place]

        rates_copy().wait_recv()
        for n in range(2):
            got, own = rates_got[n], rates_own[n]
            both_buf[n] = jnp.concatenate(
                [jnp.where(first, got, own), jnp.where(first, own, got)], axis=1
            )
        rate = both_buf[0]
        for j in range(NODES):
            phi_buf[j] = jnp.exp(rate * (-float(nodes[j])))
        node_col = jnp.concatenate([node_ref[...]] * (2 * share // LANES), axis=1)
        for m in range(modes):
            wphi_buf[m] = both_buf[1, m : m + 1, :] * jnp.exp(
                -(both_buf[0, m : m + 1, :] * node_col)
            )

    @pl.when(shares)
    def _():
        all_taps().wait_recv()
        for d in range(1, groups):
            relay_copy(block, d).start()

    @pl.when(owns)
    def _():
        rate = both_buf[0]
        decay_block = jnp.exp(rate * (-float(rows)))
        decay_one = jnp.exp(-rate)

        def advance(p, run):
            state_buf[p] = decay_one * run
            return decay_block * run + tree_sum(
                [phi_buf[j] * part_got[p, j : j + 1, :] for j in range(NODES)]
            )

        def give(targets):
            for p in targets:
                value_out[p] = tree_sum(
                    [wphi_buf[m] * state_buf[p, m : m + 1, :] for m in range(modes)]
                )

            for p in targets:
                @pl.when(here != p)
                def _():
                    value_copy(p, place).start()

        run = jnp.zeros((modes, 2 * share), F32)
        for g in range(groups):
            either(
                block == g, lambda size: all_parts(g, size).wait_recv(), inner - 1, inner
            )
            run = lax.fori_loop(g * inner, (g + 1) * inner, advance, run, unroll=4)
            if g + 1 < groups:
                state_buf[(g + 1) * inner] = decay_one * run
                give([(g + 1) * inner])
            for at in range(0, inner, 4):
                give(range(g * inner + max(1, at), g * inner + at + 4))

        value_got[place] = value_out[here]

    for n in range(5, 11):
        loads[n].wait()

    def local(q):
        for at in range(0, inner, min(8, inner)):
            cols = [
                pl.ds(pl.multiple_of((i * owners + q) * share, LANES), share)
                for i in range(at, at + min(8, inner))
            ]

            def beside(parts):
                return jnp.concatenate(list(parts), axis=1)

            signal = beside(signal_ref[:, c] for c in cols)
            spectrum = dot(forward_ref[...], jnp.concatenate([signal, signal]))
            taps = beside(taps_buf[q, at + n] for n in range(len(cols)))
            filters = jnp.concatenate([
                taps, beside(skip_ref[:, c] for c in cols),
                jnp.zeros((7, taps.shape[1]), F32),
            ])
            high, low = pieces(filters)
            response = dot(response_ref[...], jnp.concatenate([high, low, high]))
            s_re, s_im = spectrum[:rows], spectrum[rows:]
            r_re, r_im = response[:rows], response[rows:]
            product = jnp.concatenate([
                s_re * r_re - s_im * r_im, s_re * r_im + s_im * r_re,
            ])
            high, low = pieces(product)
            two = dot(inverse_ref[...], high)
            one = dot(inverse_ref[:rows], low)
            result = two[:rows] + (two[rows:] + one)
            for n, c in enumerate(cols):
                y_buf[:, c] = result[:, n * share : (n + 1) * share]

    @pl.loop(0, owners)
    def _(step):
        q = step
        if owners == groups:
            q = wrap(jnp.where(step % 2 == 0, block, twin) + step // 2 * 2, groups)

        @pl.when(q != block)
        def _():
            relay_copy(q, 0).wait_recv()

        local(q)

    @pl.when(shares)
    def _():
        all_taps().wait_send()
        for d in range(1, groups):
            relay_copy(block, d).wait_send()

    either(
        owns, lambda size: sent(part_out, size, part_send, part_recv.at[0]),
        2 * count - 1, 2 * count,
    )

    @pl.when(gives)
    def _():
        rates_copy().wait_send()

    @pl.when(here == 0)
    def _():
        value_got[...] = jnp.zeros_like(value_got)

    @pl.when(here > 0)
    def _():
        for n in range(2):
            either(
                jnp.logical_and(owns, place // count == n),
                lambda size: all_values(n, size).wait_recv(), count - 1, count,
            )

    for n in range(2):
        cols = slice(n * channels // 2, (n + 1) * channels // 2)
        value = jnp.concatenate(
            [value_got[n * count + k, :, :share] for k in range(count)]
            + [value_got[n * count + k, :, share:] for k in range(count)], axis=1
        )
        high, low = pieces(jnp.concatenate([value, jnp.zeros_like(value)]))
        carried = dot(carry_ref[...], jnp.concatenate([high, low, high]))
        gate = gating_ref[:, cols].astype(F32)
        out_ref[:, cols] = (gate * (y_buf[:, cols] + carried)).astype(BF16)

    @pl.when(owns)
    def _():
        either(
            here > 0, lambda size: sent(value_out, size, value_send, value_recv.at[0]),
            blocks - 2, blocks - 1,
        )


def per_device(signal, gating, decay_rate, residues, skip_gain):
    groups = lax.axis_size("outer")
    inner = lax.axis_size("inner")
    rows, channels = signal.shape
    width, modes = decay_rate.shape
    owners = max(1, min(groups, width // LANES))
    pair = 2 * width // owners
    held = owners * inner // 2
    blocks = groups * inner
    dma = pltpu.SemaphoreType.DMA
    nodes, constants = tables(rows)
    arguments = (
        decay_rate.T, residues.T, signal, gating, skip_gain[None, :],
        *[jnp.asarray(c) for c in constants],
    )

    return pl.pallas_call(
        functools.partial(kernel, groups, inner, owners, modes, nodes),
        out_shape=jax.ShapeDtypeStruct((rows, channels), BF16),
        in_specs=[pl.BlockSpec(memory_space=pltpu.HBM)] * len(arguments),
        out_specs=pl.BlockSpec(memory_space=pltpu.VMEM),
        scratch_shapes=[
            *[pltpu.VMEM(a.shape, a.dtype) for a in arguments],
            pltpu.VMEM((rows, channels), F32),
            pltpu.VMEM((NODES, modes, pair), F32),
            pltpu.VMEM((modes, NODES, pair), F32),
            pltpu.VMEM((NODES, pair // 2), F32),
            pltpu.VMEM((owners, inner, NODES, pair // 2), F32),
            pltpu.VMEM((held, NODES, pair), F32),
            pltpu.VMEM((blocks, NODES, pair), F32),
            pltpu.VMEM((blocks, modes, pair), F32),
            pltpu.VMEM((blocks, NODES, pair), F32),
            pltpu.VMEM((held, NODES, pair), F32),
            pltpu.VMEM((2, modes, pair // 2), F32),
            pltpu.VMEM((2, modes, pair // 2), F32),
            pltpu.VMEM((2, modes, pair), F32),
            dma((len(arguments),)),
            dma(()), dma(()), dma((groups,)), dma((owners,)),
            dma(()), dma((groups,)), dma(()), dma((2,)), dma(()), dma(()),
        ],
        compiler_params=pltpu.CompilerParams(
            collective_id=0, has_side_effects=True, vmem_limit_bytes=24 << 20
        ),
        name="modal_scan",
    )(*[pltpu.with_memory_space_constraint(a, pltpu.HBM) for a in arguments])


def solution(mesh):
    return jax.shard_map(
        per_device,
        mesh=mesh,
        in_specs=(
            P(("outer", "inner"), None),
            P(("outer", "inner"), None),
            P("inner", None),
            P("inner", None),
            P(),
        ),
        out_specs=P(("outer", "inner"), None),
        check_vma=False,
    )
```
